32 devices in a mesh: head: 4 (over x, core), ctx: 8 (over z, y).
Axes of the slice: x: 2, y: 2, z: 4, core: 2. Of those that a mesh axis runs over, the one named last changes fastest.
Arguments:
- q_in: bfloat16 [2048, 2048], P('ctx', 'head'), may hold values from -6 to 6
- k_in: bfloat16 [2048, 2048], P('ctx', 'head'), may hold values from -6 to 6
- v_in: bfloat16 [2048, 4096], P('ctx', 'head'), may hold values from -6 to 6
- gate_in: bfloat16 [2048, 4096], P('ctx', 'head'), may hold values from -6 to 6
- conv_q: float32 [4, 2048], P(None, 'head'), may hold values from -3 to 3
- conv_k: float32 [4, 2048], P(None, 'head'), may hold values from -3 to 3
- value_conv_taps: float32 [4, 4096], P(None, 'head'), may hold values from -3 to 3
- a_in: float32 [32, 2048], P('head', 'ctx'), may hold values from -4 to 12.1
- b_in: float32 [32, 2048], P('head', 'ctx'), may hold values from -5.3 to 1
- a_log: float32 [32], P('head'), may hold values from -0.92 to 0
- dt_bias: float32 [32], P('head'), may hold values from -12.5 to -3.4
- norm_gain: float32 [128], replicated, may hold values from 0.5 to 1.5
- out_weight: bfloat16 [4096, 2048], P('head'), may hold values from -0.125 to 0.125
Outputs:
- layer_out: bfloat16 [2048, 2048], P('ctx', 'head')
The draws below stay inside these ranges and needn't reach their ends.
All inputs are finite; a program needn't handle non-finite values.
Results may differ from the reference program's by a relative error of at most 0.0049.
Values may be sent and summed in bfloat16 or wider, within the bound.
A program may use at most 128 MiB of HBM per device.

```python
import jax
import jax.numpy as jnp
from jax import lax

D = 2048
KH = 16
VH = 32
DK = 128
DV = 128
CONV = 4
BLOCK = 64
TOKENS = 2048


def head_kinds(key):
    share = 0.5
    return jax.random.bernoulli(jax.random.fold_in(key, 70), share, (VH,))


def rate_offsets(key):
    quick = head_kinds(key)
    slow_vals = jax.random.uniform(jax.random.fold_in(key, 71), (VH,), jnp.float32, -12.5, -11.0)
    quick_vals = jax.random.uniform(jax.random.fold_in(key, 75), (VH,), jnp.float32, -4.2, -3.4)
    return jnp.where(quick, quick_vals, slow_vals)


def draw_dt_bias(key, part):
    return rate_offsets(key)


def draw_a_in(key, part):
    shift_amounts = rate_offsets(key)
    random_jitter = jnp.clip(jax.random.normal(jax.random.fold_in(key, 72), (VH, TOKENS), jnp.float32), -4.0, 4.0)
    chosen_places = jax.random.randint(jax.random.fold_in(key, 73), (3,), 0, TOKENS)
    token_positions = lax.broadcasted_iota(jnp.int32, (3, TOKENS), 1)
    spike_mask = jnp.any(token_positions == chosen_places[:, None], axis=0)
    raised_levels = jax.random.uniform(jax.random.fold_in(key, 74), (VH, TOKENS), jnp.float32, -1.2, -0.4)
    return jnp.where(spike_mask[None, :], raised_levels - shift_amounts[:, None], random_jitter)


def draw_b_in(key, part):
    quick = head_kinds(key)
    level = jax.random.uniform(jax.random.fold_in(key, 76), (VH, TOKENS), jnp.float32, 0.0, 1.0)
    quick_vals = -2.0 + 3.0 * level
    slow_vals = -5.3 + 2.55 * level
    return jnp.where(quick[:, None], quick_vals, slow_vals)


def with_spikes(values, rng, source, target, parts, factor):
    owner, partner = [(jnp.arange(values.shape[position]) // (values.shape[position] // parts)).reshape([-1 if axis == position else 1 for axis in range(values.ndim)]) for position in (source, target)]
    chosen = jax.random.permutation(rng, parts)[partner]
    strong = (owner == chosen) | (owner == (partner + parts // 2) % parts)
    return jnp.where(strong, factor * values, values)


def block_scale(key, shape, split, low, top_value):
    factor_of, own = 1.0, jax.random.fold_in(key, 6)
    for dim, parts in split:
        draws = jnp.exp(jax.random.uniform(jax.random.fold_in(own, dim), (parts,), jnp.float32, low / len(split), top_value / len(split)))
        factor_of = factor_of * jnp.repeat(draws, shape[dim] // parts).reshape([-1 if axis == dim else 1 for axis in range(len(shape))])
    return factor_of


def centred(own_key, shape, width, bound, cuts=(), held_as=jnp.bfloat16):
    factor_of = block_scale(own_key, shape, cuts, -0.22, 0.18) if cuts else 1.0
    result = jax.random.normal(own_key, shape, jnp.float32) * width * factor_of
    return jnp.minimum(jnp.maximum(result, -bound), bound).astype(held_as)


def heavy_noise(own_key, dims, width, reach, cuts, heavy, held_as=jnp.bfloat16):
    entries = width * jax.random.normal(own_key, dims, jnp.float32)
    if cuts:
        entries = entries * block_scale(own_key, dims, cuts, -0.22, 0.18)
    return jnp.clip(with_spikes(entries, jax.random.fold_in(own_key, 3), *heavy), -reach, reach).astype(held_as)


def setup_inputs(seed: int = 0) -> dict:
    arg_keys = jax.random.split(jax.random.key(seed), 14)
    return {
        "q_in": centred(arg_keys[0], (TOKENS, KH * DK), 1.0, 6.0, ((0, 8), (1, 4))),
        "k_in": centred(arg_keys[1], (TOKENS, KH * DK), 1.0, 6.0, ((0, 8), (1, 4))),
        "v_in": centred(arg_keys[2], (TOKENS, VH * DV), 1.0, 6.0, ((0, 8), (1, 4))),
        "gate_in": centred(arg_keys[3], (TOKENS, VH * DV), 1.0, 6.0, ((0, 8), (1, 4))),
        "conv_q": centred(arg_keys[4], (CONV, KH * DK), CONV ** -0.5, 3.0, ((1, 4),), jnp.float32),
        "conv_k": centred(arg_keys[5], (CONV, KH * DK), CONV ** -0.5, 3.0, ((1, 4),), jnp.float32),
        "value_conv_taps": centred(arg_keys[6], (CONV, VH * DV), CONV ** -0.5, 3.0, ((1, 4),), jnp.float32),
        "a_in": draw_a_in(jax.random.fold_in(arg_keys[13], 71), 0),
        "b_in": draw_b_in(jax.random.fold_in(arg_keys[13], 71), 0),
        "a_log": jnp.clip(-0.92 + 0.92 * jax.random.uniform(arg_keys[9], (VH,), jnp.float32) ** block_scale(arg_keys[9], (VH,), ((0, 4),), -0.2, 0.2), -0.92, 0.0),
        "dt_bias": draw_dt_bias(jax.random.fold_in(arg_keys[13], 71), 0),
        "norm_gain": jnp.clip(1.0 + 0.1 * jax.random.normal(arg_keys[11], (DV,), jnp.float32), 0.5, 1.5),
        "out_weight": heavy_noise(arg_keys[12], (VH * DV, D), (VH * DV) ** -0.5, 0.125, ((0, 4),), (0, 1, 4, 2.0)),
    }


def matmul_hi(left, right):
    return jnp.einsum('...ij,...jk->...ik', left, right, precision=lax.Precision.HIGHEST)

def causal_conv(inputs, prior_rows, weights):
    tap_count = weights.shape[0]
    length = inputs.shape[0]
    joined = jnp.concatenate([prior_rows, inputs], axis=0).astype(jnp.float32)
    running = weights[0] * joined[0:length]
    for offset in range(1, tap_count):
        running = running + weights[offset] * joined[offset:offset + length]
    return jax.nn.silu(running)

def unit_heads(features, head_dim):
    grouped = features.reshape(features.shape[0], -1, head_dim)
    return grouped * lax.rsqrt(lax.optimization_barrier(jnp.sum(grouped * grouped, axis=-1, keepdims=True)) + 1e-06)

def block_terms(queries, key_rows, value_rows, log_decay, strength):
    highest = lax.Precision.HIGHEST
    block_len = log_decay.shape[-1]
    cumulative = jnp.cumsum(log_decay, axis=-1)
    row_index = lax.broadcasted_iota(jnp.int32, (block_len, block_len), 0)
    col_index = lax.broadcasted_iota(jnp.int32, (block_len, block_len), 1)
    lower_mask = row_index >= col_index
    strict = row_index > col_index
    log_gap = cumulative[..., :, None] - cumulative[..., None, :]
    damping = jnp.where(lower_mask, jnp.exp(jnp.where(lower_mask, log_gap, 0.0)), 0.0)
    key_dots = jnp.einsum('...id,...jd->...ij', key_rows, key_rows, precision=highest)
    lower_part = jnp.where(strict, strength[..., :, None] * key_dots * damping, 0.0)
    identity = jnp.eye(block_len, dtype=jnp.float32)
    inverse = identity - lower_part
    power_term = lower_part
    span_len = 1
    while span_len * 2 < block_len:
        power_term = matmul_hi(power_term, power_term)
        inverse = matmul_hi(inverse, identity + power_term)
        span_len = span_len * 2
    gate_cum = jnp.exp(cumulative)
    weighted = matmul_hi(inverse, (strength * gate_cum)[..., None] * key_rows)
    pseudo = matmul_hi(inverse, strength[..., None] * value_rows)
    scores = jnp.einsum('...id,...jd->...ij', queries, key_rows, precision=highest) * damping
    query_eff = gate_cum[..., None] * queries - matmul_hi(scores, weighted)
    inside = matmul_hi(scores, pseudo)
    final_cum = cumulative[..., -1:]
    carried = jnp.exp(final_cum - cumulative)[..., None] * key_rows
    key_eye = jnp.eye(key_rows.shape[-1], dtype=jnp.float32)
    transition = jnp.exp(final_cum)[..., None] * key_eye - jnp.einsum('...cd,...ce->...de', carried, weighted, precision=highest)
    addend = jnp.einsum('...cd,...ce->...de', carried, pseudo, precision=highest)
    return (query_eff, inside, transition, addend)

def gated_norm(core, gate_in, norm_gain):
    scale_rows = lax.rsqrt(lax.optimization_barrier(jnp.mean(core * core, axis=-1, keepdims=True)) + 1e-06)
    gate_vals = gate_in.astype(jnp.float32).reshape(core.shape)
    normalized_rows = core * scale_rows * norm_gain * jax.nn.silu(gate_vals)
    return normalized_rows.astype(jnp.bfloat16).reshape(core.shape[0], -1)

def reference(q_in, k_in, v_in, gate_in, conv_q, conv_k, value_conv_taps, a_in, b_in, a_log, dt_bias, norm_gain, out_weight):
    tap_count = conv_q.shape[0]
    q_conv = causal_conv(q_in, jnp.zeros((tap_count - 1, q_in.shape[1]), jnp.bfloat16), conv_q)
    k_conv = causal_conv(k_in, jnp.zeros((tap_count - 1, k_in.shape[1]), jnp.bfloat16), conv_k)
    v_conv = causal_conv(v_in, jnp.zeros((tap_count - 1, v_in.shape[1]), jnp.bfloat16), value_conv_taps)
    queries = unit_heads(q_conv, DK) * DK ** (-0.5)
    key_dirs = unit_heads(k_conv, DK)
    log_decay = -jnp.exp(a_log)[:, None] * jax.nn.softplus(a_in + dt_bias[:, None])
    strength = jax.nn.sigmoid(b_in)
    blocks = TOKENS // BLOCK
    ratio = VH // KH
    q_blocks = queries.reshape(blocks, BLOCK, KH, DK).transpose(0, 2, 1, 3)
    k_blocks = key_dirs.reshape(blocks, BLOCK, KH, DK).transpose(0, 2, 1, 3)
    v_blocks = v_conv.reshape(blocks, BLOCK, VH, DV).transpose(0, 2, 1, 3)
    d_blocks = log_decay.reshape(VH, blocks, BLOCK).transpose(1, 0, 2)
    s_blocks = strength.reshape(VH, blocks, BLOCK).transpose(1, 0, 2)

    def advance(state, pieces):
        q_now, k_now, v_now, d_now, s_now = pieces
        q_now = jnp.repeat(q_now, ratio, axis=0)
        k_now = jnp.repeat(k_now, ratio, axis=0)
        query_eff, inside, transition, addend = block_terms(q_now, k_now, v_now, d_now, s_now)
        outputs = matmul_hi(query_eff, state) + inside
        return (matmul_hi(transition, state) + addend, outputs)
    state_zero = jnp.zeros((VH, DK, DV), jnp.float32)
    _, core = lax.scan(advance, state_zero, (q_blocks, k_blocks, v_blocks, d_blocks, s_blocks))
    core = core.transpose(0, 2, 1, 3).reshape(TOKENS, VH, DV)
    gated = gated_norm(core, gate_in, norm_gain)
    return jnp.dot(gated, out_weight, preferred_element_type=jnp.float32).astype(jnp.bfloat16)
```

```python
import functools

import jax
import jax.numpy as jnp
from jax import lax
from jax.experimental import pallas as pl
from jax.experimental.pallas import tpu as pltpu
from jax.sharding import PartitionSpec as P

KH = 16
VH = 32
DK = 128
DV = 128
RATIO = VH // KH
F32 = jnp.float32
BF16 = jnp.bfloat16
NN = (((1,), (0,)), ((), ()))
NT = (((1,), (1,)), ((), ()))
TN = (((0,), (0,)), ((), ()))


def shifted(block, axis, distance):
    devices = range(lax.axis_size(axis))
    route = [(i - distance, i) for i in devices if i - distance in devices]
    return lax.ppermute(block, axis, route)


def mm1(left, right, dims=NN):
    return lax.dot_general(left.astype(BF16), right.astype(BF16), dims, preferred_element_type=F32)


def split(x):
    high = x.astype(BF16)
    return high, (x - high.astype(F32)).astype(BF16)


def mm3(left, right, dims=NN):
    lh, ll = split(left)
    rh, rl = split(right)
    return mm1(lh, rh, dims) + (mm1(lh, rl, dims) + mm1(ll, rh, dims))


def exact_left(mask, right, dims):
    high, low = split(right)
    rest = (right - high.astype(F32) - low.astype(F32)).astype(BF16)
    return mm1(mask, high, dims) + (mm1(mask, low, dims) + mm1(mask, rest, dims))


def silu(x):
    return x / (1.0 + jnp.exp(-x))


def conv(x, halo, taps, ext):
    length, width = x.shape
    ext[0:8, :width] = jnp.zeros((8, width), F32)
    ext[5:8, :width] = halo.astype(F32)
    ext[8 : 8 + length, :width] = x.astype(F32)
    total = taps[0:1] * ext[5 : 5 + length, :width]
    for j in range(1, 4):
        total = total + taps[j : j + 1] * ext[5 + j : 5 + j + length, :width]
    return silu(total)


def unit(x):
    return x * lax.rsqrt(jnp.sum(x * x, axis=-1, keepdims=True) + 1e-06)


def local_terms(q, k, v, a2, b2, alog2, dt2):
    n = q.shape[0]
    row = lax.broadcasted_iota(jnp.int32, (n, n), 0)
    col = lax.broadcasted_iota(jnp.int32, (n, n), 1)
    lower = row >= col
    strict = row > col
    xor = row ^ col
    tri = jnp.where(lower, 1.0, 0.0)
    eye = jnp.where(row == col, 1.0, 0.0)
    x = a2 + dt2
    ld = -jnp.exp(alog2) * (jnp.maximum(x, 0.0) + jnp.log1p(jnp.exp(-jnp.abs(x))))
    strength = 1.0 / (1.0 + jnp.exp(-b2))
    ldh, ldl = split(ld)
    c_row = (
        mm1(ldh, tri, NT)
        + mm1(ldl, tri, NT)
        + mm1(ld - ldh.astype(F32) - ldl.astype(F32), tri, NT)
    )
    c_col = exact_left(tri, ld, NT)
    b_col = exact_left(eye, strength, NT)
    kk = mm3(k, k, NT)
    qk = mm3(q, k, NT)
    results = []
    for r in range(RATIO):
        cc = c_col[:, r : r + 1]
        bc = b_col[:, r : r + 1]
        gap = cc - c_row[r : r + 1, :]
        damp = jnp.where(lower, jnp.exp(jnp.minimum(gap, 0.0)), 0.0)
        low = jnp.where(strict, bc * kk * damp, 0.0)
        inv = eye - jnp.where(xor == 1, low, 0.0)
        span = 2
        while span < n:
            off = jnp.where((xor >= span) & (xor < 2 * span), low, 0.0).astype(BF16)
            inv_b = inv.astype(BF16)
            inv = inv - mm1(mm1(inv_b, off), inv_b)
            span *= 2
        inv_b = inv.astype(BF16)
        gate = jnp.exp(cc)
        rhs = jnp.concatenate([bc * gate * k, bc * v[:, r * DV : (r + 1) * DV]], axis=1)
        y = mm1(inv_b, rhs)
        y = y + mm1(inv_b, rhs - y - mm3(low, y))
        sy = mm3(qk * damp, y)
        last = cc[n - 1 : n]
        ky = mm3(jnp.exp(last - cc) * k, y, TN)
        results.append((gate * q - sy[:, :DK], sy[:, DK:], ky[:, :DK], ky[:, DK:], jnp.exp(last)))
    return results


def pick_rows(x, g):
    index = lax.broadcasted_iota(jnp.int32, x.shape, 0)
    rows = [jnp.sum(jnp.where(index == g * RATIO + r, x, 0.0), axis=0, keepdims=True) for r in range(RATIO)]
    return jnp.concatenate(rows, axis=0)


def k1_body(q_ref, k_ref, v_ref, hq_ref, hk_ref, hv_ref, cq_ref, ck_ref, cv_ref, a_ref, b_ref,
            alog_ref, dt_ref, qe_ref, o_ref, m_ref, bb_ref, ext):
    g = pl.program_id(0)
    n = q_ref.shape[0]
    q = unit(conv(q_ref[...], hq_ref[...], cq_ref[...], ext)) * DK ** (-0.5)
    k = unit(conv(k_ref[...], hk_ref[...], ck_ref[...], ext))
    v = conv(v_ref[...], hv_ref[...], cv_ref[...], ext)
    a2 = pick_rows(a_ref[...], g)
    b2 = pick_rows(b_ref[...], g)
    alog2 = jnp.concatenate([jnp.full((1, n), alog_ref[g * RATIO + r], F32) for r in range(RATIO)], axis=0)
    dt2 = jnp.concatenate([jnp.full((1, n), dt_ref[g * RATIO + r], F32) for r in range(RATIO)], axis=0)
    terms = local_terms(q, k, v, a2, b2, alog2, dt2)
    eye = jnp.where(
        lax.broadcasted_iota(jnp.int32, (DK, DK), 0) == lax.broadcasted_iota(jnp.int32, (DK, DK), 1), 1.0, 0.0
    )
    for r, (qe, o, d, bb, gl) in enumerate(terms):
        qe_ref[:, r * DV : (r + 1) * DV] = qe
        o_ref[:, r * DV : (r + 1) * DV] = o
        m_ref[r] = gl * eye - d
        bb_ref[r] = bb


def matmul_hi(left, right):
    return jnp.einsum("...ij,...jk->...ik", left, right, precision=lax.Precision.HIGHEST)


def gated_norm(core, gate_in, norm_gain):
    scale_rows = lax.rsqrt(jnp.mean(core * core, axis=-1, keepdims=True) + 1e-06)
    gate_vals = gate_in.astype(F32).reshape(core.shape)
    normalized_rows = core * scale_rows * norm_gain * jax.nn.silu(gate_vals)
    return normalized_rows.astype(BF16).reshape(core.shape[0], -1)


def local(q_in, k_in, v_in, gate_in, conv_q, conv_k, value_conv_taps, a_in, b_in, a_log, dt_bias,
          norm_gain, out_weight):
    n = q_in.shape[0]
    khl = q_in.shape[1] // DK
    vhl = v_in.shape[1] // DV
    tails = jnp.concatenate([q_in[n - 3 :], k_in[n - 3 :], v_in[n - 3 :]], axis=1)
    before = shifted(tails, "ctx", 1)
    vw = RATIO * DV
    smem = pl.BlockSpec(memory_space=pltpu.SMEM)
    qe, o, m, bb = pl.pallas_call(
        k1_body,
        grid=(khl,),
        in_specs=[
            pl.BlockSpec((n, DK), lambda g: (0, g)),
            pl.BlockSpec((n, DK), lambda g: (0, g)),
            pl.BlockSpec((n, vw), lambda g: (0, g)),
            pl.BlockSpec((3, DK), lambda g: (0, g)),
            pl.BlockSpec((3, DK), lambda g: (0, khl + g)),
            pl.BlockSpec((3, vw), lambda g: (0, khl + g)),
            pl.BlockSpec((4, DK), lambda g: (0, g)),
            pl.BlockSpec((4, DK), lambda g: (0, g)),
            pl.BlockSpec((4, vw), lambda g: (0, g)),
            pl.BlockSpec((vhl, n), lambda g: (0, 0)),
            pl.BlockSpec((vhl, n), lambda g: (0, 0)),
            smem,
            smem,
        ],
        out_specs=[
            pl.BlockSpec((n, vw), lambda g: (0, g)),
            pl.BlockSpec((n, vw), lambda g: (0, g)),
            pl.BlockSpec((RATIO, DK, DK), lambda g: (g, 0, 0)),
            pl.BlockSpec((RATIO, DK, DV), lambda g: (g, 0, 0)),
        ],
        out_shape=[
            jax.ShapeDtypeStruct((n, vhl * DV), F32),
            jax.ShapeDtypeStruct((n, vhl * DV), F32),
            jax.ShapeDtypeStruct((vhl, DK, DK), F32),
            jax.ShapeDtypeStruct((vhl, DK, DV), F32),
        ],
        scratch_shapes=[pltpu.VMEM((n + 8, vw), F32)],
        compiler_params=pltpu.CompilerParams(vmem_limit_bytes=40 << 20),
    )(q_in, k_in, v_in, before, before, before, conv_q, conv_k, value_conv_taps, a_in, b_in, a_log, dt_bias)

    def relay(index_now, incoming):
        return shifted(matmul_hi(m, incoming) + bb, "ctx", 1)

    start = lax.fori_loop(0, lax.axis_size("ctx") - 1, relay, jnp.zeros((vhl, DK, DV), F32))
    core = jnp.einsum("thd,hde->the", qe.reshape(n, vhl, DK), start, precision=lax.Precision.HIGHEST)
    core = core + o.reshape(n, vhl, DV)
    gated = gated_norm(core, gate_in, norm_gain)
    partial_sum = jnp.dot(gated, out_weight, preferred_element_type=F32)
    return lax.psum_scatter(partial_sum, "head", scatter_dimension=1, tiled=True).astype(BF16)


def solution(mesh):
    return jax.shard_map(
        local,
        mesh=mesh,
        in_specs=(
            P("ctx", "head"),
            P("ctx", "head"),
            P("ctx", "head"),
            P("ctx", "head"),
            P(None, "head"),
            P(None, "head"),
            P(None, "head"),
            P("head", "ctx"),
            P("head", "ctx"),
            P("head"),
            P("head"),
            P(),
            P("head", None),
        ),
        out_specs=P("ctx", "head"),
        check_vma=False,
    )
```

```python
import functools

import jax
import jax.numpy as jnp
from jax import lax
from jax.experimental import pallas as pl
from jax.experimental.pallas import tpu as pltpu
from jax.sharding import PartitionSpec as P

KH = 16
VH = 32
DK = 128
DV = 128
RATIO = VH // KH
F32 = jnp.float32
BF16 = jnp.bfloat16
NN = (((1,), (0,)), ((), ()))
NT = (((1,), (1,)), ((), ()))
TN = (((0,), (0,)), ((), ()))


def shifted(block, axis, distance):
    devices = range(lax.axis_size(axis))
    route = [(i - distance, i) for i in devices if i - distance in devices]
    return lax.ppermute(block, axis, route)


def mm1(left, right, dims=NN):
    return lax.dot_general(left.astype(BF16), right.astype(BF16), dims, preferred_element_type=F32)


def split(x):
    high = x.astype(BF16)
    return high, (x - high.astype(F32)).astype(BF16)


def mm3(left, right, dims=NN):
    lh, ll = split(left)
    rh, rl = split(right)
    return mm1(lh, rh, dims) + (mm1(lh, rl, dims) + mm1(ll, rh, dims))


def exact_left(mask, right, dims):
    high, low = split(right)
    rest = (right - high.astype(F32) - low.astype(F32)).astype(BF16)
    return mm1(mask, high, dims) + (mm1(mask, low, dims) + mm1(mask, rest, dims))


def silu(x):
    return x / (1.0 + jnp.exp(-x))


def conv(x, halo, taps, ext):
    length, width = x.shape
    ext[0:8, :width] = jnp.zeros((8, width), F32)
    ext[5:8, :width] = halo.astype(F32)
    ext[8 : 8 + length, :width] = x.astype(F32)
    total = taps[0:1] * ext[5 : 5 + length, :width]
    for j in range(1, 4):
        total = total + taps[j : j + 1] * ext[5 + j : 5 + j + length, :width]
    return silu(total)


def unit(x):
    return x * lax.rsqrt(jnp.sum(x * x, axis=-1, keepdims=True) + 1e-06)


def local_terms(q, k, v, a2, b2, alog2, dt2):
    n = q.shape[0]
    row = lax.broadcasted_iota(jnp.int32, (n, n), 0)
    col = lax.broadcasted_iota(jnp.int32, (n, n), 1)
    lower = row >= col
    strict = row > col
    xor = row ^ col
    tri = jnp.where(lower, 1.0, 0.0)
    eye = jnp.where(row == col, 1.0, 0.0)
    x = a2 + dt2
    ld = -jnp.exp(alog2) * (jnp.maximum(x, 0.0) + jnp.log1p(jnp.exp(-jnp.abs(x))))
    strength = 1.0 / (1.0 + jnp.exp(-b2))
    ldh, ldl = split(ld)
    c_row = (
        mm1(ldh, tri, NT)
        + mm1(ldl, tri, NT)
        + mm1(ld - ldh.astype(F32) - ldl.astype(F32), tri, NT)
    )
    c_col = exact_left(tri, ld, NT)
    b_col = exact_left(eye, strength, NT)
    kk = mm3(k, k, NT)
    qk = mm3(q, k, NT)
    results = []
    for r in range(RATIO):
        cc = c_col[:, r : r + 1]
        bc = b_col[:, r : r + 1]
        gap = cc - c_row[r : r + 1, :]
        damp = jnp.where(lower, jnp.exp(jnp.minimum(gap, 0.0)), 0.0)
        low = jnp.where(strict, bc * kk * damp, 0.0)
        inv = eye - jnp.where(xor == 1, low, 0.0)
        span = 2
        while span < n:
            off = jnp.where((xor >= span) & (xor < 2 * span), low, 0.0).astype(BF16)
            inv_b = inv.astype(BF16)
            inv = inv - mm1(mm1(inv_b, off), inv_b)
            span *= 2
        inv_b = inv.astype(BF16)
        gate = jnp.exp(cc)
        rhs = jnp.concatenate([bc * gate * k, bc * v[:, r * DV : (r + 1) * DV]], axis=1)
        y = mm1(inv_b, rhs)
        y = y + mm1(inv_b, rhs - y - mm3(low, y))
        sy = mm3(qk * damp, y)
        last = cc[n - 1 : n]
        ky = mm3(jnp.exp(last - cc) * k, y, TN)
        results.append((gate * q - sy[:, :DK], sy[:, DK:], ky[:, :DK], ky[:, DK:], jnp.exp(last)))
    return results


def pick_rows(x, g):
    index = lax.broadcasted_iota(jnp.int32, x.shape, 0)
    rows = [jnp.sum(jnp.where(index == g * RATIO + r, x, 0.0), axis=0, keepdims=True) for r in range(RATIO)]
    return jnp.concatenate(rows, axis=0)


def k1_body(q_ref, k_ref, v_ref, hq_ref, hk_ref, hv_ref, cq_ref, ck_ref, cv_ref, a_ref, b_ref,
            alog_ref, dt_ref, qe_ref, o_ref, d_ref, g_ref, bb_ref, ext):
    g = pl.program_id(0)
    n = q_ref.shape[0]
    q = unit(conv(q_ref[...], hq_ref[...], cq_ref[...], ext)) * DK ** (-0.5)
    k = unit(conv(k_ref[...], hk_ref[...], ck_ref[...], ext))
    v = conv(v_ref[...], hv_ref[...], cv_ref[...], ext)
    a2 = pick_rows(a_ref[...], g)
    b2 = pick_rows(b_ref[...], g)
    alog2 = jnp.concatenate([jnp.full((1, n), alog_ref[g * RATIO + r], F32) for r in range(RATIO)], axis=0)
    dt2 = jnp.concatenate([jnp.full((1, n), dt_ref[g * RATIO + r], F32) for r in range(RATIO)], axis=0)
    terms = local_terms(q, k, v, a2, b2, alog2, dt2)
    for r, (qe, o, d, bb, gl) in enumerate(terms):
        qe_ref[:, r * DV : (r + 1) * DV] = qe
        o_ref[:, r * DV : (r + 1) * DV] = o
        d_ref[r] = d.astype(BF16)
        g_ref[r] = jnp.broadcast_to(gl, (8, DV))
        bb_ref[r] = bb


MESH = pl.DeviceIdType.MESH


def k2_body(nh, nc, qe_ref, o_ref, d_ref, g_ref, bb_ref, gate_ref, gain_ref, w_hbm, out_ref,
            gated, w, s_in, s_out, own, p1, r1, p2, r2, w_sem, s_send, s_recv, p1_send, p1_recv, p2_send, p2_recv):
    head = lax.axis_index("head")
    ctx = lax.axis_index("ctx")
    nx = nh // 2
    x = head // 2
    core = head % 2
    mate = x * 2 + (1 - core)
    vhl = bb_ref.shape[0]
    width = out_ref.shape[1]
    peers = [((x + 1 + i) % nx) for i in range(nx)]

    barrier = pltpu.get_barrier_semaphore()
    pl.semaphore_signal(barrier, inc=1, device_id=(mate, ctx), device_id_type=MESH)
    for i in range(nx - 1):
        pl.semaphore_signal(barrier, inc=1, device_id=(peers[i] * 2 + core, ctx), device_id_type=MESH)

    @pl.when(ctx > 0)
    def _():
        pl.semaphore_signal(barrier, inc=1, device_id=(head, ctx - 1), device_id_type=MESH)

    @pl.when(ctx < nc - 1)
    def _():
        pl.semaphore_signal(barrier, inc=1, device_id=(head, ctx + 1), device_id_type=MESH)

    w_copy = pltpu.make_async_copy(w_hbm, w, w_sem)
    w_copy.start()
    neighbours = jnp.minimum(ctx, 1) + jnp.minimum(nc - 1 - ctx, 1)
    pl.semaphore_wait(barrier, nx + neighbours)

    @pl.when(ctx == 0)
    def _():
        s_in[...] = jnp.zeros_like(s_in)

    def state_copy(h):
        return pltpu.make_async_remote_copy(
            src_ref=s_out.at[h], dst_ref=s_in.at[h], send_sem=s_send.at[h], recv_sem=s_recv.at[h],
            device_id=(head, ctx + 1), device_id_type=MESH,
        )

    def one_head(h, carry):
        @pl.when(ctx > 0)
        def _():
            state_copy(h).wait_recv()

        state = s_in[h]

        @pl.when(ctx < nc - 1)
        def _():
            moved = g_ref[h][0:1, :] * state.astype(F32) - mm1(d_ref[h], state) + bb_ref[h]
            s_out[h] = moved.astype(BF16)
            state_copy(h).start()

        columns = pl.ds(pl.multiple_of(h * DV, DV), DV)
        qh, ql = split(qe_ref[:, columns])
        values = o_ref[:, columns] + (mm1(qh, state) + mm1(ql, state))
        scale = lax.rsqrt(jnp.mean(values * values, axis=-1, keepdims=True) + 1e-06)
        gated[:, columns] = (values * scale * gain_ref[...] * silu(gate_ref[:, columns].astype(F32))).astype(BF16)
        return carry

    lax.fori_loop(0, vhl, one_head, 0)
    w_copy.wait()

    def block(index):
        return mm1(gated[...], w[:, pl.ds(pl.multiple_of(index * width, 128), width)])

    def mate_copy(i):
        return pltpu.make_async_remote_copy(
            src_ref=p1.at[i], dst_ref=r1.at[i], send_sem=p1_send.at[i], recv_sem=p1_recv.at[i],
            device_id=(mate, ctx), device_id_type=MESH,
        )

    def chip_copy(i):
        return pltpu.make_async_remote_copy(
            src_ref=p2.at[i], dst_ref=r2.at[i], send_sem=p2_send.at[i], recv_sem=p2_recv.at[i],
            device_id=(peers[i] * 2 + core, ctx), device_id_type=MESH,
        )

    for i in range(nx):
        p1[i] = block(peers[i] * 2 + (1 - core)).astype(BF16)
        mate_copy(i).start()
    for i in range(nx - 1):
        own[...] = block(peers[i] * 2 + core)
        mate_copy(i).wait_recv()
        p2[i] = (own[...] + r1[i].astype(F32)).astype(BF16)
        chip_copy(i).start()
    own[...] = block(head)
    mate_copy(nx - 1).wait_recv()
    total = own[...] + r1[nx - 1].astype(F32)
    for i in range(nx - 1):
        chip_copy(i).wait_recv()
        total = total + r2[i].astype(F32)
    out_ref[...] = total.astype(BF16)
    for i in range(nx):
        mate_copy(i).wait_send()
    for i in range(nx - 1):
        chip_copy(i).wait_send()

    @pl.when(ctx < nc - 1)
    def _():
        def drain(h, carry):
            state_copy(h).wait_send()
            return carry

        lax.fori_loop(0, vhl, drain, 0)


def local(q_in, k_in, v_in, gate_in, conv_q, conv_k, value_conv_taps, a_in, b_in, a_log, dt_bias,
          norm_gain, out_weight):
    n = q_in.shape[0]
    khl = q_in.shape[1] // DK
    vhl = v_in.shape[1] // DV
    tails = jnp.concatenate([q_in[n - 3 :], k_in[n - 3 :], v_in[n - 3 :]], axis=1)
    before = shifted(tails, "ctx", 1)
    vw = RATIO * DV
    smem = pl.BlockSpec(memory_space=pltpu.SMEM)
    qe, o, d, g_last, bb = pl.pallas_call(
        k1_body,
        grid=(khl,),
        in_specs=[
            pl.BlockSpec((n, DK), lambda g: (0, g)),
            pl.BlockSpec((n, DK), lambda g: (0, g)),
            pl.BlockSpec((n, vw), lambda g: (0, g)),
            pl.BlockSpec((3, DK), lambda g: (0, g)),
            pl.BlockSpec((3, DK), lambda g: (0, khl + g)),
            pl.BlockSpec((3, vw), lambda g: (0, khl + g)),
            pl.BlockSpec((4, DK), lambda g: (0, g)),
            pl.BlockSpec((4, DK), lambda g: (0, g)),
            pl.BlockSpec((4, vw), lambda g: (0, g)),
            pl.BlockSpec((vhl, n), lambda g: (0, 0)),
            pl.BlockSpec((vhl, n), lambda g: (0, 0)),
            smem,
            smem,
        ],
        out_specs=[
            pl.BlockSpec((n, vw), lambda g: (0, g)),
            pl.BlockSpec((n, vw), lambda g: (0, g)),
            pl.BlockSpec((RATIO, DK, DK), lambda g: (g, 0, 0)),
            pl.BlockSpec((RATIO, 8, DV), lambda g: (g, 0, 0)),
            pl.BlockSpec((RATIO, DK, DV), lambda g: (g, 0, 0)),
        ],
        out_shape=[
            jax.ShapeDtypeStruct((n, vhl * DV), F32),
            jax.ShapeDtypeStruct((n, vhl * DV), F32),
            jax.ShapeDtypeStruct((vhl, DK, DK), BF16),
            jax.ShapeDtypeStruct((vhl, 8, DV), F32),
            jax.ShapeDtypeStruct((vhl, DK, DV), F32),
        ],
        scratch_shapes=[pltpu.VMEM((n + 8, vw), F32)],
        compiler_params=pltpu.CompilerParams(vmem_limit_bytes=40 << 20),
    )(q_in, k_in, v_in, before, before, before, conv_q, conv_k, value_conv_taps, a_in, b_in, a_log, dt_bias)

    nh = lax.axis_size("head")
    nc = lax.axis_size("ctx")
    nx = nh // 2
    rows, total_width = out_weight.shape
    width = total_width // nh
    vmem = pl.BlockSpec(memory_space=pltpu.VMEM)
    dma = pltpu.SemaphoreType.DMA
    return pl.pallas_call(
        functools.partial(k2_body, nh, nc),
        in_specs=[vmem] * 7 + [pl.BlockSpec(memory_space=pl.ANY)],
        out_specs=vmem,
        out_shape=jax.ShapeDtypeStruct((n, width), BF16),
        scratch_shapes=[
            pltpu.VMEM((n, vhl * DV), BF16),
            pltpu.VMEM((rows, total_width), BF16),
            pltpu.VMEM((vhl, DK, DV), BF16),
            pltpu.VMEM((vhl, DK, DV), BF16),
            pltpu.VMEM((n, width), F32),
            pltpu.VMEM((nx, n, width), BF16),
            pltpu.VMEM((nx, n, width), BF16),
            pltpu.VMEM((nx - 1, n, width), BF16),
            pltpu.VMEM((nx - 1, n, width), BF16),
            dma,
            dma((vhl,)),
            dma((vhl,)),
            dma((nx,)),
            dma((nx,)),
            dma((nx - 1,)),
            dma((nx - 1,)),
        ],
        compiler_params=pltpu.CompilerParams(
            collective_id=0, has_side_effects=True, vmem_limit_bytes=40 << 20
        ),
    )(qe, o, d, g_last, bb, gate_in, norm_gain.reshape(1, DV), out_weight)


def solution(mesh):
    return jax.shard_map(
        local,
        mesh=mesh,
        in_specs=(
            P("ctx", "head"),
            P("ctx", "head"),
            P("ctx", "head"),
            P("ctx", "head"),
            P(None, "head"),
            P(None, "head"),
            P(None, "head"),
            P("head", "ctx"),
            P("head", "ctx"),
            P("head"),
            P("head"),
            P(),
            P("head", None),
        ),
        out_specs=P("ctx", "head"),
        check_vma=False,
    )
```

```python
import functools

import jax
import jax.numpy as jnp
from jax import lax
from jax.experimental import pallas as pl
from jax.experimental.pallas import tpu as pltpu
from jax.sharding import PartitionSpec as P

KH = 16
VH = 32
DK = 128
DV = 128
RATIO = VH // KH
SIDE = 128
F32 = jnp.float32
BF16 = jnp.bfloat16
NN = (((1,), (0,)), ((), ()))
NT = (((1,), (1,)), ((), ()))
TN = (((0,), (0,)), ((), ()))


def mm1(left, right, dims=NN):
    return lax.dot_general(left.astype(BF16), right.astype(BF16), dims, preferred_element_type=F32)


def split(x):
    high = x.astype(BF16)
    return high, (x - high.astype(F32)).astype(BF16)


def mm3(left, right, dims=NN):
    lh, ll = split(left)
    rh, rl = split(right)
    return mm1(lh, rh, dims) + (mm1(lh, rl, dims) + mm1(ll, rh, dims))


def exact_left(mask, right, dims):
    high, low = split(right)
    rest = (right - high.astype(F32) - low.astype(F32)).astype(BF16)
    return mm1(mask, high, dims) + (mm1(mask, low, dims) + mm1(mask, rest, dims))


def silu(x):
    return x / (1.0 + jnp.exp(-x))


def conv(x, halo, taps, ext):
    length, width = x.shape
    ext[0:8, :width] = halo.astype(F32)[8:16]
    ext[8 : 8 + length, :width] = x.astype(F32)
    total = taps[0:1] * ext[5 : 5 + length, :width]
    for j in range(1, 4):
        total = total + taps[j : j + 1] * ext[5 + j : 5 + j + length, :width]
    return silu(total)


def unit(x):
    return x * lax.rsqrt(jnp.sum(x * x, axis=-1, keepdims=True) + 1e-06)


def pick_row(x, h):
    index = lax.broadcasted_iota(jnp.int32, x.shape, 0)
    return jnp.sum(jnp.where(index == h, x, 0.0), axis=0, keepdims=True)


def local_terms(heads, ld, strength):
    n = heads[0][0].shape[0]
    nb = n // SIDE
    row = lax.broadcasted_iota(jnp.int32, (n, n), 0)
    col = lax.broadcasted_iota(jnp.int32, (n, n), 1)
    tri = jnp.where(row >= col, 1.0, 0.0).astype(BF16)
    diag = jnp.where(row == col, 1.0, 0.0).astype(BF16)
    l0, l1 = split(ld)
    l2 = (ld - l0.astype(F32) - l1.astype(F32)).astype(BF16)
    c_row = mm1(l0, tri, NT) + mm1(l1, tri, NT) + mm1(l2, tri, NT)
    c_col = exact_left(tri, ld, NT)
    b_col = exact_left(diag, strength, NT)
    brow = lax.broadcasted_iota(jnp.int32, (SIDE, SIDE), 0)
    bcol = lax.broadcasted_iota(jnp.int32, (SIDE, SIDE), 1)
    xor = jnp.where(brow > bcol, brow ^ bcol, 0)
    level = jnp.where(xor > 0, 0, -1)
    span = 2
    while span < SIDE:
        level = level + jnp.where(xor >= span, 1, 0)
        span *= 2
    lower = brow >= bcol
    eye = jnp.where(brow == bcol, 1.0, 0.0)

    def part(i):
        return slice(i * SIDE, (i + 1) * SIDE)

    items = []
    for g, (q, k, v) in enumerate(heads):
        kk = mm1(k, k, NT)
        qk = mm3(q, k, NT)
        for r in range(RATIO):
            h = g * RATIO + r
            cc = c_col[:, h : h + 1]
            bc = b_col[:, h : h + 1]
            low, scores = {}, {}
            for i in range(nb):
                for j in range(i + 1):
                    gap = jnp.minimum(cc[part(i)] - c_row[h : h + 1, part(j)], 0.0)
                    damp = jnp.exp(gap)
                    lo = bc[part(i)] * kk[part(i), part(j)] * damp
                    sc = qk[part(i), part(j)] * damp
                    if i == j:
                        lo = jnp.where(level >= 0, lo, 0.0)
                        sc = jnp.where(lower, sc, 0.0)
                    low[i, j] = lo
                    scores[i, j] = sc
            gate = jnp.exp(cc)
            rhs = jnp.concatenate([bc * gate * k, bc * v[:, r * DV : (r + 1) * DV]], axis=1)
            items.append((q, k, cc, gate, low, scores, rhs))

    blocks = [low[i, i] for (_, _, _, _, low, _, _) in items for i in range(nb)]
    inverses = [eye - jnp.where(level == 0, block, 0.0) for block in blocks]
    depth = 1
    while (1 << depth) < SIDE:
        held = [inv.astype(BF16) for inv in inverses]
        first = [mm1(hb, jnp.where(level == depth, block, 0.0)) for hb, block in zip(held, blocks)]
        inverses = [inv - mm1(p, hb) for inv, p, hb in zip(inverses, first, held)]
        depth += 1
    held = [inv.astype(BF16) for inv in inverses]

    solved = [[] for _ in items]
    for i in range(nb):
        targets = []
        for t, (_, _, _, _, low, _, rhs) in enumerate(items):
            target = rhs[part(i)]
            for j in range(i):
                target = target - mm1(low[i, j], solved[t][j])
            targets.append(target)
        guess = [mm1(held[t * nb + i], target) for t, target in enumerate(targets)]
        rest = [
            target - y - mm1(items[t][4][i, i], y) for t, (target, y) in enumerate(zip(targets, guess))
        ]
        for t in range(len(items)):
            solved[t].append(guess[t] + mm1(held[t * nb + i], rest[t]))

    results = []
    for t, (q, k, cc, gate, _, scores, _) in enumerate(items):
        y = jnp.concatenate(solved[t], axis=0)
        yh, yl = split(y)
        outs = []
        for i in range(nb):
            sc = jnp.concatenate([scores[i, j] for j in range(i + 1)], axis=1)
            sh, sl = split(sc)
            top = (i + 1) * SIDE
            outs.append(mm1(sh, yh[:top]) + (mm1(sh, yl[:top]) + mm1(sl, yh[:top])))
        sy = jnp.concatenate(outs, axis=0)
        last = cc[n - 1 : n]
        kh, kl = split(jnp.exp(last - cc) * k)
        ky = mm1(kh, yh, TN) + (mm1(kh, yl, TN) + mm1(kl, yh, TN))
        results.append((gate * q - sy[:, :DK], sy[:, DK:], ky[:, :DK], ky[:, DK:], jnp.exp(last)))
    return results


MESH = pl.DeviceIdType.MESH


def body(nh, nc, alog_ref, dt_ref, q_hbm, k_hbm, v_hbm, cq_hbm, ck_hbm, cv_hbm, a_hbm, b_hbm,
         gate_hbm, gain_hbm, w_hbm, out_ref,
         q_ref, k_ref, v_ref, cq_ref, ck_ref, cv_ref, a_ref, b_ref, gate_ref, gain_ref, w,
         hq, hk, hv, ext, qe_ref, o_ref, d_ref, g_ref, bb_ref,
         gated, s_in, s_out, own, p1, r1, p2, r2,
         in_sem, h_send, h_recv, s_send, s_recv, p1_send, p1_recv, p2_send, p2_recv):
    head = lax.axis_index("head")
    ctx = lax.axis_index("ctx")
    nx = nh // 2
    x = head // 2
    core = head % 2
    mate = x * 2 + (1 - core)
    n = q_ref.shape[0]
    khl = q_ref.shape[1] // DK
    vhl = khl * RATIO
    width = out_ref.shape[1]
    peers = [((x + 1 + i) % nx) for i in range(nx)]

    barrier = pltpu.get_barrier_semaphore()
    pl.semaphore_signal(barrier, inc=1, device_id=(mate, ctx), device_id_type=MESH)
    for i in range(nx - 1):
        pl.semaphore_signal(barrier, inc=1, device_id=(peers[i] * 2 + core, ctx), device_id_type=MESH)

    @pl.when(ctx > 0)
    def _():
        pl.semaphore_signal(barrier, inc=1, device_id=(head, ctx - 1), device_id_type=MESH)

    @pl.when(ctx < nc - 1)
    def _():
        pl.semaphore_signal(barrier, inc=1, device_id=(head, ctx + 1), device_id_type=MESH)

    pairs = [
        (q_hbm, q_ref), (k_hbm, k_ref), (v_hbm, v_ref), (cq_hbm, cq_ref), (ck_hbm, ck_ref), (cv_hbm, cv_ref),
        (a_hbm, a_ref), (b_hbm, b_ref), (gate_hbm, gate_ref), (gain_hbm, gain_ref), (w_hbm, w),
    ]
    loads = [pltpu.make_async_copy(src, dst, in_sem.at[i]) for i, (src, dst) in enumerate(pairs)]
    for load in loads:
        load.start()

    neighbours = jnp.minimum(ctx, 1) + jnp.minimum(nc - 1 - ctx, 1)
    pl.semaphore_wait(barrier, nx + neighbours)

    halos = [
        pltpu.make_async_remote_copy(
            src_ref=src.at[pl.ds(n - 16, 16)], dst_ref=dst, send_sem=h_send.at[i], recv_sem=h_recv.at[i],
            device_id=(head, ctx + 1), device_id_type=MESH,
        )
        for i, (src, dst) in enumerate([(q_hbm, hq), (k_hbm, hk), (v_hbm, hv)])
    ]

    @pl.when(ctx < nc - 1)
    def _():
        for halo in halos:
            halo.start()

    @pl.when(ctx == 0)
    def _():
        hq[...] = jnp.zeros_like(hq)
        hk[...] = jnp.zeros_like(hk)
        hv[...] = jnp.zeros_like(hv)
        s_in[...] = jnp.zeros_like(s_in)

    for load in loads[:8]:
        load.wait()

    @pl.when(ctx > 0)
    def _():
        for halo in halos:
            halo.wait_recv()

    group = 2 if khl % 2 == 0 else 1
    vw = RATIO * DV

    def local_step(step, carry):
        heads, lds, strengths = [], [], []
        for t in range(group):
            g = step * group + t
            kc = pl.ds(pl.multiple_of(g * DK, DK), DK)
            vc = pl.ds(pl.multiple_of(g * vw, vw), vw)
            q = unit(conv(q_ref[:, kc], hq[:, kc], cq_ref[:, kc], ext)) * DK ** (-0.5)
            k = unit(conv(k_ref[:, kc], hk[:, kc], ck_ref[:, kc], ext))
            v = conv(v_ref[:, vc], hv[:, vc], cv_ref[:, vc], ext)
            heads.append((q, k, v))
            for r in range(RATIO):
                h = g * RATIO + r
                ax = pick_row(a_ref[...], h) + dt_ref[h]
                rate = jnp.exp(jnp.full((1, n), alog_ref[h], F32))
                lds.append(-rate * (jnp.maximum(ax, 0.0) + jnp.log1p(jnp.exp(-jnp.abs(ax)))))
                strengths.append(1.0 / (1.0 + jnp.exp(-pick_row(b_ref[...], h))))
        terms = local_terms(heads, jnp.concatenate(lds, axis=0), jnp.concatenate(strengths, axis=0))
        for t, (qe, o, d, bb, gl) in enumerate(terms):
            h = step * (group * RATIO) + t
            columns = pl.ds(pl.multiple_of(h * DV, DV), DV)
            qe_ref[:, columns] = qe
            o_ref[:, columns] = o
            d_ref[h] = d.astype(BF16)
            g_ref[h] = jnp.broadcast_to(gl, (8, DV))
            bb_ref[h] = bb
        return carry

    lax.fori_loop(0, khl // group, local_step, 0)

    for load in loads[8:10]:
        load.wait()

    def state_copy(p):
        both = pl.ds(p * RATIO, RATIO)
        return pltpu.make_async_remote_copy(
            src_ref=s_out.at[both], dst_ref=s_in.at[both], send_sem=s_send.at[p], recv_sem=s_recv.at[p],
            device_id=(head, ctx + 1), device_id_type=MESH,
        )

    def one_pair(p, carry):
        @pl.when(ctx > 0)
        def _():
            state_copy(p).wait_recv()

        @pl.when(ctx < nc - 1)
        def _():
            for r in range(RATIO):
                h = p * RATIO + r
                state = s_in[h]
                moved = g_ref[h][0:1, :] * state.astype(F32) - mm1(d_ref[h], state) + bb_ref[h]
                s_out[h] = moved.astype(BF16)
            state_copy(p).start()

        for r in range(RATIO):
            h = p * RATIO + r
            state = s_in[h]
            columns = pl.ds(pl.multiple_of(h * DV, DV), DV)
            qh, ql = split(qe_ref[:, columns])
            values = o_ref[:, columns] + (mm1(qh, state) + mm1(ql, state))
            scale = lax.rsqrt(jnp.mean(values * values, axis=-1, keepdims=True) + 1e-06)
            gate = silu(gate_ref[:, columns].astype(F32))
            gated[:, columns] = (values * scale * gain_ref[...] * gate).astype(BF16)
        return carry

    lax.fori_loop(0, khl, one_pair, 0)
    loads[10].wait()

    def block(index):
        return mm1(gated[...], w[:, pl.ds(pl.multiple_of(index * width, 128), width)])

    def mate_copy(i):
        return pltpu.make_async_remote_copy(
            src_ref=p1.at[i], dst_ref=r1.at[i], send_sem=p1_send.at[i], recv_sem=p1_recv.at[i],
            device_id=(mate, ctx), device_id_type=MESH,
        )

    def chip_copy(i):
        return pltpu.make_async_remote_copy(
            src_ref=p2.at[i], dst_ref=r2.at[i], send_sem=p2_send.at[i], recv_sem=p2_recv.at[i],
            device_id=(peers[i] * 2 + core, ctx), device_id_type=MESH,
        )

    for i in range(nx):
        p1[i] = block(peers[i] * 2 + (1 - core)).astype(BF16)
        mate_copy(i).start()
    for i in range(nx - 1):
        own[...] = block(peers[i] * 2 + core)
        mate_copy(i).wait_recv()
        p2[i] = (own[...] + r1[i].astype(F32)).astype(BF16)
        chip_copy(i).start()
    own[...] = block(head)
    mate_copy(nx - 1).wait_recv()
    total = own[...] + r1[nx - 1].astype(F32)
    for i in range(nx - 1):
        chip_copy(i).wait_recv()
        total = total + r2[i].astype(F32)
    out_ref[...] = total.astype(BF16)
    for i in range(nx):
        mate_copy(i).wait_send()
    for i in range(nx - 1):
        chip_copy(i).wait_send()

    @pl.when(ctx < nc - 1)
    def _():
        def drain(h, carry):
            state_copy(h).wait_send()
            return carry

        lax.fori_loop(0, khl, drain, 0)
        for halo in halos:
            halo.wait_send()


def local(q_in, k_in, v_in, gate_in, conv_q, conv_k, value_conv_taps, a_in, b_in, a_log, dt_bias,
          norm_gain, out_weight):
    n = q_in.shape[0]
    khl = q_in.shape[1] // DK
    vhl = khl * RATIO
    nh = lax.axis_size("head")
    nc = lax.axis_size("ctx")
    nx = nh // 2
    rows, total_width = out_weight.shape
    width = total_width // nh
    smem = pl.BlockSpec(memory_space=pltpu.SMEM)
    hbm = pl.BlockSpec(memory_space=pltpu.HBM)
    dma = pltpu.SemaphoreType.DMA
    operands = (q_in, k_in, v_in, conv_q, conv_k, value_conv_taps, a_in, b_in, gate_in,
                norm_gain.reshape(1, DV), out_weight)
    vmem = pltpu.VMEM
    return pl.pallas_call(
        functools.partial(body, nh, nc),
        in_specs=[smem, smem] + [hbm] * len(operands),
        out_specs=pl.BlockSpec(memory_space=pltpu.VMEM),
        out_shape=jax.ShapeDtypeStruct((n, width), BF16),
        scratch_shapes=[vmem(op.shape, op.dtype) for op in operands] + [
            vmem((16, q_in.shape[1]), BF16),
            vmem((16, k_in.shape[1]), BF16),
            vmem((16, v_in.shape[1]), BF16),
            vmem((n + 8, RATIO * DV), F32),
            vmem((n, vhl * DK), F32),
            vmem((n, vhl * DV), F32),
            vmem((vhl, DK, DK), BF16),
            vmem((vhl, 8, DV), F32),
            vmem((vhl, DK, DV), F32),
            vmem((n, vhl * DV), BF16),
            vmem((vhl, DK, DV), BF16),
            vmem((vhl, DK, DV), BF16),
            vmem((n, width), F32),
            vmem((nx, n, width), BF16),
            vmem((nx, n, width), BF16),
            vmem((nx - 1, n, width), BF16),
            vmem((nx - 1, n, width), BF16),
            dma((len(operands),)),
            dma((3,)),
            dma((3,)),
            dma((khl,)),
            dma((khl,)),
            dma((nx,)),
            dma((nx,)),
            dma((nx - 1,)),
            dma((nx - 1,)),
        ],
        compiler_params=pltpu.CompilerParams(
            collective_id=0, has_side_effects=True, vmem_limit_bytes=63 << 20
        ),
    )(a_log, dt_bias, *operands)


def solution(mesh):
    return jax.shard_map(
        local,
        mesh=mesh,
        in_specs=(
            P("ctx", "head"),
            P("ctx", "head"),
            P("ctx", "head"),
            P("ctx", "head"),
            P(None, "head"),
            P(None, "head"),
            P(None, "head"),
            P("head", "ctx"),
            P("head", "ctx"),
            P("head"),
            P("head"),
            P(),
            P("head", None),
        ),
        out_specs=P("ctx", "head"),
        check_vma=False,
    )
```

```python
import functools

import jax
import jax.numpy as jnp
from jax import lax
from jax.experimental import pallas as pl
from jax.experimental.pallas import tpu as pltpu
from jax.sharding import PartitionSpec as P

KH = 16
VH = 32
DK = 128
DV = 128
RATIO = VH // KH
SIDE = 128
F32 = jnp.float32
BF16 = jnp.bfloat16
NN = (((1,), (0,)), ((), ()))
NT = (((1,), (1,)), ((), ()))
TN = (((0,), (0,)), ((), ()))


def mm1(left, right, dims=NN):
    return lax.dot_general(left.astype(BF16), right.astype(BF16), dims, preferred_element_type=F32)


def split(x):
    high = x.astype(BF16)
    return high, (x - high.astype(F32)).astype(BF16)


def mm3(left, right, dims=NN):
    lh, ll = split(left)
    rh, rl = split(right)
    return mm1(lh, rh, dims) + (mm1(lh, rl, dims) + mm1(ll, rh, dims))


def exact_left(mask, right, dims):
    high, low = split(right)
    rest = (right - high.astype(F32) - low.astype(F32)).astype(BF16)
    return mm1(mask, high, dims) + (mm1(mask, low, dims) + mm1(mask, rest, dims))


def silu(x):
    return x / (1.0 + jnp.exp(-x))


def conv(x, halo, taps, ext):
    length, width = x.shape
    ext[0:8, :width] = halo.astype(F32)[8:16]
    ext[8 : 8 + length, :width] = x.astype(F32)
    total = taps[0:1] * ext[5 : 5 + length, :width]
    for j in range(1, 4):
        total = total + taps[j : j + 1] * ext[5 + j : 5 + j + length, :width]
    return silu(total)


def unit(x):
    return x * lax.rsqrt(jnp.sum(x * x, axis=-1, keepdims=True) + 1e-06)


def pick_row(x, h):
    index = lax.broadcasted_iota(jnp.int32, x.shape, 0)
    return jnp.sum(jnp.where(index == h, x, 0.0), axis=0, keepdims=True)


def local_terms(heads, ld, strength):
    n = heads[0][0].shape[0]
    nb = n // SIDE
    row = lax.broadcasted_iota(jnp.int32, (n, n), 0)
    col = lax.broadcasted_iota(jnp.int32, (n, n), 1)
    tri = jnp.where(row >= col, 1.0, 0.0).astype(BF16)
    diag = jnp.where(row == col, 1.0, 0.0).astype(BF16)
    l0, l1 = split(ld)
    l2 = (ld - l0.astype(F32) - l1.astype(F32)).astype(BF16)
    c_row = mm1(l0, tri, NT) + mm1(l1, tri, NT) + mm1(l2, tri, NT)
    c_col = exact_left(tri, ld, NT)
    b_col = exact_left(diag, strength, NT)
    brow = lax.broadcasted_iota(jnp.int32, (SIDE, SIDE), 0)
    bcol = lax.broadcasted_iota(jnp.int32, (SIDE, SIDE), 1)
    xor = jnp.where(brow > bcol, brow ^ bcol, 0)
    level = jnp.where(xor > 0, 0, -1)
    span = 2
    while span < SIDE:
        level = level + jnp.where(xor >= span, 1, 0)
        span *= 2
    lower = brow >= bcol
    eye = jnp.where(brow == bcol, 1.0, 0.0)

    def part(i):
        return slice(i * SIDE, (i + 1) * SIDE)

    items = []
    for g, (q, k, v) in enumerate(heads):
        kk = mm1(k, k, NT)
        qk = mm3(q, k, NT)
        for r in range(RATIO):
            h = g * RATIO + r
            cc = c_col[:, h : h + 1]
            bc = b_col[:, h : h + 1]
            low, scores = {}, {}
            for i in range(nb):
                for j in range(i + 1):
                    gap = jnp.minimum(cc[part(i)] - c_row[h : h + 1, part(j)], 0.0)
                    damp = jnp.exp(gap)
                    lo = bc[part(i)] * kk[part(i), part(j)] * damp
                    sc = qk[part(i), part(j)] * damp
                    if i == j:
                        lo = jnp.where(level >= 0, lo, 0.0)
                        sc = jnp.where(lower, sc, 0.0)
                    low[i, j] = lo
                    scores[i, j] = sc
            gate = jnp.exp(cc)
            rhs = jnp.concatenate([bc * gate * k, bc * v[:, r * DV : (r + 1) * DV]], axis=1)
            items.append((q, k, cc, gate, low, scores, rhs))

    blocks = [low[i, i] for (_, _, _, _, low, _, _) in items for i in range(nb)]
    inverses = [eye - jnp.where(level == 0, block, 0.0) for block in blocks]
    depth = 1
    while (1 << depth) < SIDE:
        held = [inv.astype(BF16) for inv in inverses]
        first = [mm1(hb, jnp.where(level == depth, block, 0.0)) for hb, block in zip(held, blocks)]
        inverses = [inv - mm1(p, hb) for inv, p, hb in zip(inverses, first, held)]
        depth += 1
    held = [inv.astype(BF16) for inv in inverses]

    solved = [[] for _ in items]
    for i in range(nb):
        targets = []
        for t, (_, _, _, _, low, _, rhs) in enumerate(items):
            target = rhs[part(i)]
            for j in range(i):
                target = target - mm1(low[i, j], solved[t][j])
            targets.append(target)
        guess = [mm1(held[t * nb + i], target) for t, target in enumerate(targets)]
        rest = [
            target - y - mm1(items[t][4][i, i], y) for t, (target, y) in enumerate(zip(targets, guess))
        ]
        for t in range(len(items)):
            solved[t].append(guess[t] + mm1(held[t * nb + i], rest[t]))

    results = []
    for t, (q, k, cc, gate, _, scores, _) in enumerate(items):
        y = jnp.concatenate(solved[t], axis=0)
        yh, yl = split(y)
        outs = []
        for i in range(nb):
            sc = jnp.concatenate([scores[i, j] for j in range(i + 1)], axis=1)
            top = (i + 1) * SIDE
            outs.append(mm1(sc, yh[:top]) + mm1(sc, yl[:top]))
        sy = jnp.concatenate(outs, axis=0)
        last = cc[n - 1 : n]
        kh = (jnp.exp(last - cc) * k).astype(BF16)
        ky = mm1(kh, yh, TN) + mm1(kh, yl, TN)
        results.append((gate * q - sy[:, :DK], sy[:, DK:], ky[:, :DK], ky[:, DK:], jnp.exp(last)))
    return results


MESH = pl.DeviceIdType.MESH


def body(nh, nc, alog_ref, dt_ref, q_hbm, k_hbm, v_hbm, cq_hbm, ck_hbm, cv_hbm, a_hbm, b_hbm,
         gate_hbm, gain_hbm, w_hbm, out_ref,
         q_ref, k_ref, v_ref, cq_ref, ck_ref, cv_ref, a_ref, b_ref, gate_ref, gain_ref, w,
         hq, hk, hv, ext, qe_ref, o_ref, d_ref, g_ref, bb_ref,
         gated, acc, s_in, s_out, own, p1, r1, p2, r2,
         in_sem, h_send, h_recv, s_send, s_recv, p1_send, p1_recv, p2_send, p2_recv):
    head = lax.axis_index("head")
    ctx = lax.axis_index("ctx")
    nx = nh // 2
    x = head // 2
    core = head % 2
    mate = x * 2 + (1 - core)
    n = q_ref.shape[0]
    khl = q_ref.shape[1] // DK
    vhl = khl * RATIO
    width = out_ref.shape[1]
    peers = [((x + 1 + i) % nx) for i in range(nx)]

    barrier = pltpu.get_barrier_semaphore()
    pl.semaphore_signal(barrier, inc=1, device_id=(mate, ctx), device_id_type=MESH)
    for i in range(nx - 1):
        pl.semaphore_signal(barrier, inc=1, device_id=(peers[i] * 2 + core, ctx), device_id_type=MESH)

    @pl.when(ctx > 0)
    def _():
        pl.semaphore_signal(barrier, inc=1, device_id=(head, ctx - 1), device_id_type=MESH)

    @pl.when(ctx < nc - 1)
    def _():
        pl.semaphore_signal(barrier, inc=1, device_id=(head, ctx + 1), device_id_type=MESH)

    pairs = [
        (q_hbm, q_ref), (k_hbm, k_ref), (v_hbm, v_ref), (cq_hbm, cq_ref), (ck_hbm, ck_ref), (cv_hbm, cv_ref),
        (a_hbm, a_ref), (b_hbm, b_ref), (gate_hbm, gate_ref), (gain_hbm, gain_ref), (w_hbm, w),
    ]
    loads = [pltpu.make_async_copy(src, dst, in_sem.at[i]) for i, (src, dst) in enumerate(pairs)]
    for load in loads:
        load.start()

    neighbours = jnp.minimum(ctx, 1) + jnp.minimum(nc - 1 - ctx, 1)
    pl.semaphore_wait(barrier, nx + neighbours)

    halos = [
        pltpu.make_async_remote_copy(
            src_ref=src.at[pl.ds(n - 16, 16)], dst_ref=dst, send_sem=h_send.at[i], recv_sem=h_recv.at[i],
            device_id=(head, ctx + 1), device_id_type=MESH,
        )
        for i, (src, dst) in enumerate([(q_hbm, hq), (k_hbm, hk), (v_hbm, hv)])
    ]

    @pl.when(ctx < nc - 1)
    def _():
        for halo in halos:
            halo.start()

    @pl.when(ctx == 0)
    def _():
        hq[...] = jnp.zeros_like(hq)
        hk[...] = jnp.zeros_like(hk)
        hv[...] = jnp.zeros_like(hv)
        s_in[...] = jnp.zeros_like(s_in)

    for load in loads[:8]:
        load.wait()

    @pl.when(ctx > 0)
    def _():
        for halo in halos:
            halo.wait_recv()

    group = 2 if khl % 2 == 0 else 1
    vw = RATIO * DV

    def local_step(step, carry):
        heads, lds, strengths = [], [], []
        for t in range(group):
            g = step * group + t
            kc = pl.ds(pl.multiple_of(g * DK, DK), DK)
            vc = pl.ds(pl.multiple_of(g * vw, vw), vw)
            q = unit(conv(q_ref[:, kc], hq[:, kc], cq_ref[:, kc], ext)) * DK ** (-0.5)
            k = unit(conv(k_ref[:, kc], hk[:, kc], ck_ref[:, kc], ext))
            v = conv(v_ref[:, vc], hv[:, vc], cv_ref[:, vc], ext)
            heads.append((q, k, v))
            for r in range(RATIO):
                h = g * RATIO + r
                ax = pick_row(a_ref[...], h) + dt_ref[h]
                rate = jnp.exp(jnp.full((1, n), alog_ref[h], F32))
                lds.append(-rate * (jnp.maximum(ax, 0.0) + jnp.log1p(jnp.exp(-jnp.abs(ax)))))
                strengths.append(1.0 / (1.0 + jnp.exp(-pick_row(b_ref[...], h))))
        terms = local_terms(heads, jnp.concatenate(lds, axis=0), jnp.concatenate(strengths, axis=0))
        for t, (qe, o, d, bb, gl) in enumerate(terms):
            h = step * (group * RATIO) + t
            columns = pl.ds(pl.multiple_of(h * DV, DV), DV)
            qe_ref[:, columns] = qe
            o_ref[:, columns] = o
            d_ref[h] = d.astype(BF16)
            g_ref[h] = jnp.broadcast_to(gl, (8, DV))
            bb_ref[h] = bb
        return carry

    lax.fori_loop(0, khl // group, local_step, 0)

    for load in loads[8:10]:
        load.wait()

    def state_copy(h):
        return pltpu.make_async_remote_copy(
            src_ref=s_out.at[h], dst_ref=s_in.at[h], send_sem=s_send.at[h], recv_sem=s_recv.at[h],
            device_id=(head, ctx + 1), device_id_type=MESH,
        )

    @pl.when(ctx < nc - 1)
    def _():
        def relay(h, carry):
            @pl.when(ctx > 0)
            def _():
                state_copy(h).wait_recv()

            state = s_in[h]
            moved = (g_ref[h][0:1, :] * state.astype(F32) + bb_ref[h]) - mm1(d_ref[h], state)
            s_out[h] = moved.astype(BF16)
            state_copy(h).start()
            return carry

        lax.fori_loop(0, vhl, relay, 0)

    loads[10].wait()

    def finish_pair(p):
        @pl.when(ctx == nc - 1)
        def _():
            for r in range(RATIO):
                state_copy(p * RATIO + r).wait_recv()

        for r in range(RATIO):
            h = p * RATIO + r
            state = s_in[h]
            columns = pl.ds(h * DV if isinstance(h, int) else pl.multiple_of(h * DV, DV), DV)
            qh, ql = split(qe_ref[:, columns])
            values = o_ref[:, columns] + (mm1(qh, state) + mm1(ql, state))
            scale = lax.rsqrt(jnp.mean(values * values, axis=-1, keepdims=True) + 1e-06)
            gate = silu(gate_ref[:, columns].astype(F32))
            gated[:, r * DV : (r + 1) * DV] = (values * scale * gain_ref[...] * gate).astype(BF16)

    def add_pair(p, carry):
        finish_pair(p)
        rows = pl.ds(pl.multiple_of(p * vw, vw), vw)
        for j in range(nh):
            cols = slice(j * width, (j + 1) * width)
            acc[:, cols] = acc[:, cols] + mm1(gated[...], w[rows, cols])
        return carry

    acc[...] = jnp.zeros_like(acc)
    lax.fori_loop(0, khl - 1, add_pair, 0)
    finish_pair(khl - 1)

    def block(index):
        cols = pl.ds(pl.multiple_of(index * width, 128), width)
        return acc[:, cols] + mm1(gated[...], w[pl.ds((khl - 1) * vw, vw), cols])

    def mate_copy(i):
        return pltpu.make_async_remote_copy(
            src_ref=p1.at[i], dst_ref=r1.at[i], send_sem=p1_send.at[i], recv_sem=p1_recv.at[i],
            device_id=(mate, ctx), device_id_type=MESH,
        )

    def chip_copy(i):
        return pltpu.make_async_remote_copy(
            src_ref=p2.at[i], dst_ref=r2.at[i], send_sem=p2_send.at[i], recv_sem=p2_recv.at[i],
            device_id=(peers[i] * 2 + core, ctx), device_id_type=MESH,
        )

    for i in range(nx):
        p1[i] = block(peers[i] * 2 + (1 - core)).astype(BF16)
        mate_copy(i).start()
    for i in range(nx - 1):
        own[...] = block(peers[i] * 2 + core)
        mate_copy(i).wait_recv()
        p2[i] = (own[...] + r1[i].astype(F32)).astype(BF16)
        chip_copy(i).start()
    own[...] = block(head)
    mate_copy(nx - 1).wait_recv()
    total = own[...] + r1[nx - 1].astype(F32)
    for i in range(nx - 1):
        chip_copy(i).wait_recv()
        total = total + r2[i].astype(F32)
    out_ref[...] = total.astype(BF16)
    for i in range(nx):
        mate_copy(i).wait_send()
    for i in range(nx - 1):
        chip_copy(i).wait_send()

    @pl.when(ctx < nc - 1)
    def _():
        def drain(h, carry):
            state_copy(h).wait_send()
            return carry

        lax.fori_loop(0, vhl, drain, 0)
        for halo in halos:
            halo.wait_send()


def local(q_in, k_in, v_in, gate_in, conv_q, conv_k, value_conv_taps, a_in, b_in, a_log, dt_bias,
          norm_gain, out_weight):
    n = q_in.shape[0]
    khl = q_in.shape[1] // DK
    vhl = khl * RATIO
    nh = lax.axis_size("head")
    nc = lax.axis_size("ctx")
    nx = nh // 2
    rows, total_width = out_weight.shape
    width = total_width // nh
    smem = pl.BlockSpec(memory_space=pltpu.SMEM)
    hbm = pl.BlockSpec(memory_space=pltpu.HBM)
    dma = pltpu.SemaphoreType.DMA
    operands = (q_in, k_in, v_in, conv_q, conv_k, value_conv_taps, a_in, b_in, gate_in,
                norm_gain.reshape(1, DV), out_weight)
    vmem = pltpu.VMEM
    return pl.pallas_call(
        functools.partial(body, nh, nc),
        in_specs=[smem, smem] + [hbm] * len(operands),
        out_specs=pl.BlockSpec(memory_space=pltpu.VMEM),
        out_shape=jax.ShapeDtypeStruct((n, width), BF16),
        scratch_shapes=[vmem(op.shape, op.dtype) for op in operands] + [
            vmem((16, q_in.shape[1]), BF16),
            vmem((16, k_in.shape[1]), BF16),
            vmem((16, v_in.shape[1]), BF16),
            vmem((n + 8, RATIO * DV), F32),
            vmem((n, vhl * DK), F32),
            vmem((n, vhl * DV), F32),
            vmem((vhl, DK, DK), BF16),
            vmem((vhl, 8, DV), F32),
            vmem((vhl, DK, DV), F32),
            vmem((n, RATIO * DV), BF16),
            vmem((n, total_width), F32),
            vmem((vhl, DK, DV), BF16),
            vmem((vhl, DK, DV), BF16),
            vmem((n, width), F32),
            vmem((nx, n, width), BF16),
            vmem((nx, n, width), BF16),
            vmem((nx - 1, n, width), BF16),
            vmem((nx - 1, n, width), BF16),
            dma((len(operands),)),
            dma((3,)),
            dma((3,)),
            dma((vhl,)),
            dma((vhl,)),
            dma((nx,)),
            dma((nx,)),
            dma((nx - 1,)),
            dma((nx - 1,)),
        ],
        compiler_params=pltpu.CompilerParams(
            collective_id=0, has_side_effects=True, vmem_limit_bytes=63 << 20
        ),
    )(a_log, dt_bias, *operands)


def solution(mesh):
    return jax.shard_map(
        local,
        mesh=mesh,
        in_specs=(
            P("ctx", "head"),
            P("ctx", "head"),
            P("ctx", "head"),
            P("ctx", "head"),
            P(None, "head"),
            P(None, "head"),
            P(None, "head"),
            P("head", "ctx"),
            P("head", "ctx"),
            P("head"),
            P("head"),
            P(),
            P("head", None),
        ),
        out_specs=P("ctx", "head"),
        check_vma=False,
    )
```

```python
import functools

import jax
import jax.numpy as jnp
from jax import lax
from jax.experimental import pallas as pl
from jax.experimental.pallas import tpu as pltpu
from jax.sharding import PartitionSpec as P

KH = 16
VH = 32
DK = 128
DV = 128
RATIO = VH // KH
SIDE = 128
F32 = jnp.float32
BF16 = jnp.bfloat16
NN = (((1,), (0,)), ((), ()))
NT = (((1,), (1,)), ((), ()))
TN = (((0,), (0,)), ((), ()))


def mm1(left, right, dims=NN):
    return lax.dot_general(left.astype(BF16), right.astype(BF16), dims, preferred_element_type=F32)


def split(x):
    high = x.astype(BF16)
    return high, (x - high.astype(F32)).astype(BF16)


def mm3(left, right, dims=NN):
    lh, ll = split(left)
    rh, rl = split(right)
    return mm1(lh, rh, dims) + (mm1(lh, rl, dims) + mm1(ll, rh, dims))


def exact_left(mask, right, dims):
    high, low = split(right)
    rest = (right - high.astype(F32) - low.astype(F32)).astype(BF16)
    return mm1(mask, high, dims) + (mm1(mask, low, dims) + mm1(mask, rest, dims))


def silu(x):
    return x / (1.0 + jnp.exp(-x))


def conv(x, halo, taps, ext):
    length, width = x.shape
    ext[0:8, :width] = halo.astype(F32)[8:16]
    ext[8 : 8 + length, :width] = x.astype(F32)
    total = taps[0:1] * ext[5 : 5 + length, :width]
    for j in range(1, 4):
        total = total + taps[j : j + 1] * ext[5 + j : 5 + j + length, :width]
    return silu(total)


def unit(x):
    return x * lax.rsqrt(jnp.sum(x * x, axis=-1, keepdims=True) + 1e-06)


def pick_row(x, h):
    index = lax.broadcasted_iota(jnp.int32, x.shape, 0)
    return jnp.sum(jnp.where(index == h, x, 0.0), axis=0, keepdims=True)


def local_terms(heads, ld, strength):
    n = heads[0][0].shape[0]
    nb = n // SIDE
    row = lax.broadcasted_iota(jnp.int32, (n, n), 0)
    col = lax.broadcasted_iota(jnp.int32, (n, n), 1)
    tri = jnp.where(row >= col, 1.0, 0.0).astype(BF16)
    diag = jnp.where(row == col, 1.0, 0.0).astype(BF16)
    l0, l1 = split(ld)
    l2 = (ld - l0.astype(F32) - l1.astype(F32)).astype(BF16)
    c_row = mm1(l0, tri, NT) + mm1(l1, tri, NT) + mm1(l2, tri, NT)
    c_col = exact_left(tri, ld, NT)
    b_col = exact_left(diag, strength, NT)
    brow = lax.broadcasted_iota(jnp.int32, (SIDE, SIDE), 0)
    bcol = lax.broadcasted_iota(jnp.int32, (SIDE, SIDE), 1)
    xor = jnp.where(brow > bcol, brow ^ bcol, 0)
    level = jnp.where(xor > 0, 0, -1)
    span = 2
    while span < SIDE:
        level = level + jnp.where(xor >= span, 1, 0)
        span *= 2
    lower = brow >= bcol
    eye = jnp.where(brow == bcol, 1.0, 0.0)

    def part(i):
        return slice(i * SIDE, (i + 1) * SIDE)

    items = []
    for g, (q, k, v) in enumerate(heads):
        kk = mm1(k, k, NT)
        qk = mm3(q, k, NT)
        for r in range(RATIO):
            h = g * RATIO + r
            cc = c_col[:, h : h + 1]
            bc = b_col[:, h : h + 1]
            low, scores = {}, {}
            for i in range(nb):
                for j in range(i + 1):
                    gap = jnp.minimum(cc[part(i)] - c_row[h : h + 1, part(j)], 0.0)
                    damp = jnp.exp(gap)
                    lo = bc[part(i)] * kk[part(i), part(j)] * damp
                    sc = qk[part(i), part(j)] * damp
                    if i == j:
                        lo = jnp.where(level >= 0, lo, 0.0)
                        sc = jnp.where(lower, sc, 0.0)
                    low[i, j] = lo
                    scores[i, j] = sc
            gate = jnp.exp(cc)
            rhs = jnp.concatenate([bc * gate * k, bc * v[:, r * DV : (r + 1) * DV]], axis=1)
            items.append((q, k, cc, gate, low, scores, rhs))

    blocks = [low[i, i] for (_, _, _, _, low, _, _) in items for i in range(nb)]
    inverses = [eye - jnp.where(level == 0, block, 0.0) for block in blocks]
    depth = 1
    while (1 << depth) < SIDE:
        held = [inv.astype(BF16) for inv in inverses]
        first = [mm1(hb, jnp.where(level == depth, block, 0.0)) for hb, block in zip(held, blocks)]
        inverses = [inv - mm1(p, hb) for inv, p, hb in zip(inverses, first, held)]
        depth += 1
    held = [inv.astype(BF16) for inv in inverses]

    solved = [[] for _ in items]
    for i in range(nb):
        targets = []
        for t, (_, _, _, _, low, _, rhs) in enumerate(items):
            target = rhs[part(i)]
            for j in range(i):
                target = target - mm1(low[i, j], solved[t][j])
            targets.append(target)
        guess = [mm1(held[t * nb + i], target) for t, target in enumerate(targets)]
        rest = [
            target - y - mm1(items[t][4][i, i], y) for t, (target, y) in enumerate(zip(targets, guess))
        ]
        for t in range(len(items)):
            solved[t].append(guess[t] + mm1(held[t * nb + i], rest[t]))

    results = []
    for t, (q, k, cc, gate, _, scores, _) in enumerate(items):
        y = jnp.concatenate(solved[t], axis=0)
        yh, yl = split(y)
        outs = []
        for i in range(nb):
            sc = jnp.concatenate([scores[i, j] for j in range(i + 1)], axis=1)
            top = (i + 1) * SIDE
            outs.append(mm1(sc, yh[:top]) + mm1(sc, yl[:top]))
        sy = jnp.concatenate(outs, axis=0)
        last = cc[n - 1 : n]
        kh = (jnp.exp(last - cc) * k).astype(BF16)
        ky = mm1(kh, yh, TN) + mm1(kh, yl, TN)
        results.append((gate * q - sy[:, :DK], sy[:, DK:], ky[:, :DK], ky[:, DK:], jnp.exp(last)))
    return results


MESH = pl.DeviceIdType.MESH


def body(nh, nc, alog_ref, dt_ref, q_hbm, k_hbm, v_hbm, cq_hbm, ck_hbm, cv_hbm, a_hbm, b_hbm,
         gate_hbm, gain_hbm, w_hbm, out_ref,
         q_ref, k_ref, v_ref, cq_ref, ck_ref, cv_ref, a_ref, b_ref, gate_ref, gain_ref, w,
         hq, hk, hv, ext, qe_ref, o_ref, d_ref, g_ref, bb_ref,
         gated, acc, s_in, s_out, f_out, db, pdb, pg, own, p1, r1, p2, r2,
         in_sem, h_send, h_recv, s_send, s_recv, f_send, f_recv, e_send, e_recv, p1_send, p1_recv, p2_send, p2_recv):
    head = lax.axis_index("head")
    ctx = lax.axis_index("ctx")
    nx = nh // 2
    x = head // 2
    core = head % 2
    mate = x * 2 + (1 - core)
    n = q_ref.shape[0]
    khl = q_ref.shape[1] // DK
    vhl = khl * RATIO
    width = out_ref.shape[1]
    peers = [((x + 1 + i) % nx) for i in range(nx)]

    barrier = pltpu.get_barrier_semaphore()
    pl.semaphore_signal(barrier, inc=1, device_id=(mate, ctx), device_id_type=MESH)
    for i in range(nx - 1):
        pl.semaphore_signal(barrier, inc=1, device_id=(peers[i] * 2 + core, ctx), device_id_type=MESH)

    @pl.when(ctx > 0)
    def _():
        pl.semaphore_signal(barrier, inc=1, device_id=(head, ctx - 1), device_id_type=MESH)

    @pl.when(ctx < nc - 1)
    def _():
        pl.semaphore_signal(barrier, inc=1, device_id=(head, ctx + 1), device_id_type=MESH)

    even = ctx % 2 == 0

    @pl.when(jnp.logical_and(even, ctx > 1))
    def _():
        pl.semaphore_signal(barrier, inc=1, device_id=(head, ctx - 2), device_id_type=MESH)

    @pl.when(jnp.logical_and(even, ctx < nc - 2))
    def _():
        pl.semaphore_signal(barrier, inc=1, device_id=(head, ctx + 2), device_id_type=MESH)

    pairs = [
        (q_hbm, q_ref), (k_hbm, k_ref), (v_hbm, v_ref), (cq_hbm, cq_ref), (ck_hbm, ck_ref), (cv_hbm, cv_ref),
        (a_hbm, a_ref), (b_hbm, b_ref), (gate_hbm, gate_ref), (gain_hbm, gain_ref), (w_hbm, w),
    ]
    loads = [pltpu.make_async_copy(src, dst, in_sem.at[i]) for i, (src, dst) in enumerate(pairs)]
    for load in loads:
        load.start()

    neighbours = jnp.minimum(ctx, 1) + jnp.minimum(nc - 1 - ctx, 1)
    seconds = (1 - ctx % 2) * (jnp.minimum(ctx // 2, 1) + jnp.minimum((nc - 1 - ctx) // 2, 1))
    pl.semaphore_wait(barrier, nx + neighbours + seconds)

    halos = [
        pltpu.make_async_remote_copy(
            src_ref=src.at[pl.ds(n - 16, 16)], dst_ref=dst, send_sem=h_send.at[i], recv_sem=h_recv.at[i],
            device_id=(head, ctx + 1), device_id_type=MESH,
        )
        for i, (src, dst) in enumerate([(q_hbm, hq), (k_hbm, hk), (v_hbm, hv)])
    ]

    @pl.when(ctx < nc - 1)
    def _():
        for halo in halos:
            halo.start()

    @pl.when(ctx == 0)
    def _():
        hq[...] = jnp.zeros_like(hq)
        hk[...] = jnp.zeros_like(hk)
        hv[...] = jnp.zeros_like(hv)
        s_in[...] = jnp.zeros_like(s_in)

    for load in loads[:8]:
        load.wait()

    @pl.when(ctx > 0)
    def _():
        for halo in halos:
            halo.wait_recv()

    group = 2 if khl % 2 == 0 else 1
    vw = RATIO * DV

    per_step = group * RATIO

    def pair_copies(step):
        some = pl.ds(step * per_step, per_step)
        return [
            pltpu.make_async_remote_copy(
                src_ref=src.at[some], dst_ref=dst.at[some], send_sem=e_send.at[i, step], recv_sem=e_recv.at[i, step],
                device_id=(head, ctx - 1), device_id_type=MESH,
            )
            for i, (src, dst) in enumerate([(db, pdb), (g_ref, pg)])
        ]

    gives = jnp.logical_and(jnp.logical_not(even), ctx < nc - 1)
    composes = jnp.logical_and(even, ctx < nc - 2)

    def local_step(step, carry):
        heads, lds, strengths = [], [], []
        for t in range(group):
            g = step * group + t
            kc = pl.ds(pl.multiple_of(g * DK, DK), DK)
            vc = pl.ds(pl.multiple_of(g * vw, vw), vw)
            q = unit(conv(q_ref[:, kc], hq[:, kc], cq_ref[:, kc], ext)) * DK ** (-0.5)
            k = unit(conv(k_ref[:, kc], hk[:, kc], ck_ref[:, kc], ext))
            v = conv(v_ref[:, vc], hv[:, vc], cv_ref[:, vc], ext)
            heads.append((q, k, v))
            for r in range(RATIO):
                h = g * RATIO + r
                ax = pick_row(a_ref[...], h) + dt_ref[h]
                rate = jnp.exp(jnp.full((1, n), alog_ref[h], F32))
                lds.append(-rate * (jnp.maximum(ax, 0.0) + jnp.log1p(jnp.exp(-jnp.abs(ax)))))
                strengths.append(1.0 / (1.0 + jnp.exp(-pick_row(b_ref[...], h))))
        terms = local_terms(heads, jnp.concatenate(lds, axis=0), jnp.concatenate(strengths, axis=0))
        for t, (qe, o, d, bb, gl) in enumerate(terms):
            h = step * (group * RATIO) + t
            columns = pl.ds(pl.multiple_of(h * DV, DV), DV)
            qe_ref[:, columns] = qe
            o_ref[:, columns] = o
            d_ref[h] = d
            g_ref[h] = jnp.broadcast_to(gl, (8, DV))
            bb_ref[h] = bb
            db[h] = jnp.concatenate([d, bb], axis=1).astype(BF16)

        @pl.when(gives)
        def _():
            for copy in pair_copies(step):
                copy.start()

        return carry

    lax.fori_loop(0, khl // group, local_step, 0)

    for load in loads[8:10]:
        load.wait()

    def state_copy(h):
        return pltpu.make_async_remote_copy(
            src_ref=s_out.at[h], dst_ref=s_in.at[h], send_sem=s_send.at[h], recv_sem=s_recv.at[h],
            device_id=(head, ctx + 1), device_id_type=MESH,
        )

    def forward_copy(h):
        return pltpu.make_async_remote_copy(
            src_ref=f_out.at[h], dst_ref=s_in.at[h], send_sem=f_send.at[h], recv_sem=f_recv.at[h],
            device_id=(head, ctx + 2), device_id_type=MESH,
        )

    def relay_step(step, carry):
        @pl.when(composes)
        def _():
            for copy in pair_copies(step):
                copy.wait_recv()

        def relay(t, inner):
            h = step * per_step + t
            g0 = g_ref[h][0:1, :]

            @pl.when(composes)
            def _():
                g1 = pg[h][0:1, :]
                later = pdb[h]
                d1 = later[:, :DK]
                both = mm1(d1, db[h])
                pair_d = (g1 * d_ref[h] + g0 * d1.astype(F32) - both[:, :DK]).astype(BF16)
                pair_b = later[:, DK:].astype(F32) + g1 * bb_ref[h] - both[:, DK:]

                @pl.when(ctx > 0)
                def _():
                    forward_copy(h).wait_recv()

                state = s_in[h]
                moved = (g1 * g0 * state.astype(F32) + pair_b) - mm1(pair_d, state)
                f_out[h] = moved.astype(BF16)
                forward_copy(h).start()

            @pl.when(ctx == nc - 2)
            def _():
                if nc > 2:
                    forward_copy(h).wait_recv()

            state = s_in[h]
            moved = (g0 * state.astype(F32) + bb_ref[h]) - mm1(db[h][:, :DK], state)
            s_out[h] = moved.astype(BF16)
            state_copy(h).start()
            return inner

        return lax.fori_loop(0, per_step, relay, carry)

    @pl.when(even)
    def _():
        lax.fori_loop(0, khl // group, relay_step, 0)

    loads[10].wait()

    def finish_pair(p):
        @pl.when(jnp.logical_not(even))
        def _():
            for r in range(RATIO):
                state_copy(p * RATIO + r).wait_recv()

        for r in range(RATIO):
            h = p * RATIO + r
            state = s_in[h]
            columns = pl.ds(h * DV if isinstance(h, int) else pl.multiple_of(h * DV, DV), DV)
            qh, ql = split(qe_ref[:, columns])
            values = o_ref[:, columns] + (mm1(qh, state) + mm1(ql, state))
            scale = lax.rsqrt(jnp.mean(values * values, axis=-1, keepdims=True) + 1e-06)
            gate = silu(gate_ref[:, columns].astype(F32))
            gated[:, r * DV : (r + 1) * DV] = (values * scale * gain_ref[...] * gate).astype(BF16)

    def add_pair(p, carry):
        finish_pair(p)
        rows = pl.ds(pl.multiple_of(p * vw, vw), vw)
        for j in range(nh):
            cols = slice(j * width, (j + 1) * width)
            acc[:, cols] = acc[:, cols] + mm1(gated[...], w[rows, cols])
        return carry

    acc[...] = jnp.zeros_like(acc)
    lax.fori_loop(0, khl - 1, add_pair, 0)
    finish_pair(khl - 1)

    def block(index):
        cols = pl.ds(pl.multiple_of(index * width, 128), width)
        return acc[:, cols] + mm1(gated[...], w[pl.ds((khl - 1) * vw, vw), cols])

    def mate_copy(i):
        return pltpu.make_async_remote_copy(
            src_ref=p1.at[i], dst_ref=r1.at[i], send_sem=p1_send.at[i], recv_sem=p1_recv.at[i],
            device_id=(mate, ctx), device_id_type=MESH,
        )

    def chip_copy(i):
        return pltpu.make_async_remote_copy(
            src_ref=p2.at[i], dst_ref=r2.at[i], send_sem=p2_send.at[i], recv_sem=p2_recv.at[i],
            device_id=(peers[i] * 2 + core, ctx), device_id_type=MESH,
        )

    for i in range(nx):
        p1[i] = block(peers[i] * 2 + (1 - core)).astype(BF16)
        mate_copy(i).start()
    for i in range(nx - 1):
        own[...] = block(peers[i] * 2 + core)
        mate_copy(i).wait_recv()
        p2[i] = (own[...] + r1[i].astype(F32)).astype(BF16)
        chip_copy(i).start()
    own[...] = block(head)
    mate_copy(nx - 1).wait_recv()
    total = own[...] + r1[nx - 1].astype(F32)
    for i in range(nx - 1):
        chip_copy(i).wait_recv()
        total = total + r2[i].astype(F32)
    out_ref[...] = total.astype(BF16)
    for i in range(nx):
        mate_copy(i).wait_send()
    for i in range(nx - 1):
        chip_copy(i).wait_send()

    @pl.when(ctx < nc - 1)
    def _():
        for halo in halos:
            halo.wait_send()

    @pl.when(even)
    def _():
        def drain(h, carry):
            state_copy(h).wait_send()
            return carry

        lax.fori_loop(0, vhl, drain, 0)

    @pl.when(composes)
    def _():
        def drain(h, carry):
            forward_copy(h).wait_send()
            return carry

        lax.fori_loop(0, vhl, drain, 0)

    @pl.when(gives)
    def _():
        for step in range(khl // group):
            for copy in pair_copies(step):
                copy.wait_send()


def local(q_in, k_in, v_in, gate_in, conv_q, conv_k, value_conv_taps, a_in, b_in, a_log, dt_bias,
          norm_gain, out_weight):
    n = q_in.shape[0]
    khl = q_in.shape[1] // DK
    vhl = khl * RATIO
    nh = lax.axis_size("head")
    nc = lax.axis_size("ctx")
    nx = nh // 2
    rows, total_width = out_weight.shape
    width = total_width // nh
    smem = pl.BlockSpec(memory_space=pltpu.SMEM)
    hbm = pl.BlockSpec(memory_space=pltpu.HBM)
    dma = pltpu.SemaphoreType.DMA
    operands = (q_in, k_in, v_in, conv_q, conv_k, value_conv_taps, a_in, b_in, gate_in,
                norm_gain.reshape(1, DV), out_weight)
    vmem = pltpu.VMEM
    return pl.pallas_call(
        functools.partial(body, nh, nc),
        in_specs=[smem, smem] + [hbm] * len(operands),
        out_specs=pl.BlockSpec(memory_space=pltpu.VMEM),
        out_shape=jax.ShapeDtypeStruct((n, width), BF16),
        scratch_shapes=[vmem(op.shape, op.dtype) for op in operands] + [
            vmem((16, q_in.shape[1]), BF16),
            vmem((16, k_in.shape[1]), BF16),
            vmem((16, v_in.shape[1]), BF16),
            vmem((n + 8, RATIO * DV), F32),
            vmem((n, vhl * DK), F32),
            vmem((n, vhl * DV), F32),
            vmem((vhl, DK, DK), F32),
            vmem((vhl, 8, DV), F32),
            vmem((vhl, DK, DV), F32),
            vmem((n, RATIO * DV), BF16),
            vmem((n, total_width), F32),
            vmem((vhl, DK, DV), BF16),
            vmem((vhl, DK, DV), BF16),
            vmem((vhl, DK, DV), BF16),
            vmem((vhl, DK, DK + DV), BF16),
            vmem((vhl, DK, DK + DV), BF16),
            vmem((vhl, 8, DV), F32),
            vmem((n, width), F32),
            vmem((nx, n, width), BF16),
            vmem((nx, n, width), BF16),
            vmem((nx - 1, n, width), BF16),
            vmem((nx - 1, n, width), BF16),
            dma((len(operands),)),
            dma((3,)),
            dma((3,)),
            dma((vhl,)),
            dma((vhl,)),
            dma((vhl,)),
            dma((vhl,)),
            dma((2, khl)),
            dma((2, khl)),
            dma((nx,)),
            dma((nx,)),
            dma((nx - 1,)),
            dma((nx - 1,)),
        ],
        compiler_params=pltpu.CompilerParams(
            collective_id=0, has_side_effects=True, vmem_limit_bytes=63 << 20
        ),
    )(a_log, dt_bias, *operands)


def solution(mesh):
    return jax.shard_map(
        local,
        mesh=mesh,
        in_specs=(
            P("ctx", "head"),
            P("ctx", "head"),
            P("ctx", "head"),
            P("ctx", "head"),
            P(None, "head"),
            P(None, "head"),
            P(None, "head"),
            P("head", "ctx"),
            P("head", "ctx"),
            P("head"),
            P("head"),
            P(),
            P("head", None),
        ),
        out_specs=P("ctx", "head"),
        check_vma=False,
    )
```

```python
import functools

import jax
import jax.numpy as jnp
from jax import lax
from jax.experimental import pallas as pl
from jax.experimental.pallas import tpu as pltpu
from jax.sharding import PartitionSpec as P

KH = 16
VH = 32
DK = 128
DV = 128
RATIO = VH // KH
SIDE = 128
F32 = jnp.float32
BF16 = jnp.bfloat16
NN = (((1,), (0,)), ((), ()))
NT = (((1,), (1,)), ((), ()))
TN = (((0,), (0,)), ((), ()))


def mm1(left, right, dims=NN):
    return lax.dot_general(left.astype(BF16), right.astype(BF16), dims, preferred_element_type=F32)


def split(x):
    high = x.astype(BF16)
    return high, (x - high.astype(F32)).astype(BF16)


def mm3(left, right, dims=NN):
    lh, ll = split(left)
    rh, rl = split(right)
    return mm1(lh, rh, dims) + (mm1(lh, rl, dims) + mm1(ll, rh, dims))


def exact_left(mask, right, dims):
    high, low = split(right)
    rest = (right - high.astype(F32) - low.astype(F32)).astype(BF16)
    return mm1(mask, high, dims) + (mm1(mask, low, dims) + mm1(mask, rest, dims))


def silu(x):
    return x / (1.0 + jnp.exp(-x))


def conv(x, halo, taps, ext):
    length, width = x.shape
    ext[0:8, :width] = halo.astype(F32)[8:16]
    ext[8 : 8 + length, :width] = x.astype(F32)
    total = taps[0:1] * ext[5 : 5 + length, :width]
    for j in range(1, 4):
        total = total + taps[j : j + 1] * ext[5 + j : 5 + j + length, :width]
    return silu(total)


def unit(x):
    return x * lax.rsqrt(jnp.sum(x * x, axis=-1, keepdims=True) + 1e-06)


def pick_row(x, h):
    index = lax.broadcasted_iota(jnp.int32, x.shape, 0)
    return jnp.sum(jnp.where(index == h, x, 0.0), axis=0, keepdims=True)


def local_terms(heads, ld, strength):
    n = heads[0][0].shape[0]
    nb = n // SIDE
    row = lax.broadcasted_iota(jnp.int32, (n, n), 0)
    col = lax.broadcasted_iota(jnp.int32, (n, n), 1)
    tri = jnp.where(row >= col, 1.0, 0.0).astype(BF16)
    diag = jnp.where(row == col, 1.0, 0.0).astype(BF16)
    l0, l1 = split(ld)
    l2 = (ld - l0.astype(F32) - l1.astype(F32)).astype(BF16)
    c_row = mm1(l0, tri, NT) + mm1(l1, tri, NT) + mm1(l2, tri, NT)
    c_col = exact_left(tri, ld, NT)
    b_col = exact_left(diag, strength, NT)
    brow = lax.broadcasted_iota(jnp.int32, (SIDE, SIDE), 0)
    bcol = lax.broadcasted_iota(jnp.int32, (SIDE, SIDE), 1)
    xor = jnp.where(brow > bcol, brow ^ bcol, 0)
    level = jnp.where(xor > 0, 0, -1)
    span = 2
    while span < SIDE:
        level = level + jnp.where(xor >= span, 1, 0)
        span *= 2
    lower = brow >= bcol
    eye = jnp.where(brow == bcol, 1.0, 0.0)

    def part(i):
        return slice(i * SIDE, (i + 1) * SIDE)

    items = []
    for g, (q, k, v) in enumerate(heads):
        kk = mm1(k, k, NT)
        qk = mm3(q, k, NT)
        for r in range(RATIO):
            h = g * RATIO + r
            cc = c_col[:, h : h + 1]
            bc = b_col[:, h : h + 1]
            low, scores = {}, {}
            for i in range(nb):
                for j in range(i + 1):
                    gap = jnp.minimum(cc[part(i)] - c_row[h : h + 1, part(j)], 0.0)
                    damp = jnp.exp(gap)
                    lo = bc[part(i)] * kk[part(i), part(j)] * damp
                    sc = qk[part(i), part(j)] * damp
                    if i == j:
                        lo = jnp.where(level >= 0, lo, 0.0)
                        sc = jnp.where(lower, sc, 0.0)
                    low[i, j] = lo
                    scores[i, j] = sc
            gate = jnp.exp(cc)
            rhs = jnp.concatenate([bc * gate * k, bc * v[:, r * DV : (r + 1) * DV]], axis=1)
            items.append((q, k, cc, gate, low, scores, rhs))

    blocks = [low[i, i] for (_, _, _, _, low, _, _) in items for i in range(nb)]
    inverses = [eye - jnp.where(level == 0, block, 0.0) for block in blocks]
    depth = 1
    while (1 << depth) < SIDE:
        held = [inv.astype(BF16) for inv in inverses]
        first = [mm1(hb, jnp.where(level == depth, block, 0.0)) for hb, block in zip(held, blocks)]
        inverses = [inv - mm1(p, hb) for inv, p, hb in zip(inverses, first, held)]
        depth += 1
    held = [inv.astype(BF16) for inv in inverses]

    solved = [[] for _ in items]
    for i in range(nb):
        targets = []
        for t, (_, _, _, _, low, _, rhs) in enumerate(items):
            target = rhs[part(i)]
            for j in range(i):
                target = target - mm1(low[i, j], solved[t][j])
            targets.append(target)
        guess = [mm1(held[t * nb + i], target) for t, target in enumerate(targets)]
        rest = [
            target - y - mm1(items[t][4][i, i], y) for t, (target, y) in enumerate(zip(targets, guess))
        ]
        for t in range(len(items)):
            solved[t].append(guess[t] + mm1(held[t * nb + i], rest[t]))

    results = []
    for t, (q, k, cc, gate, _, scores, _) in enumerate(items):
        y = jnp.concatenate(solved[t], axis=0)
        yh, yl = split(y)
        outs = []
        for i in range(nb):
            sc = jnp.concatenate([scores[i, j] for j in range(i + 1)], axis=1)
            top = (i + 1) * SIDE
            outs.append(mm1(sc, yh[:top]) + mm1(sc, yl[:top]))
        sy = jnp.concatenate(outs, axis=0)
        last = cc[n - 1 : n]
        kh = (jnp.exp(last - cc) * k).astype(BF16)
        ky = mm1(kh, yh, TN) + mm1(kh, yl, TN)
        results.append((gate * q - sy[:, :DK], sy[:, DK:], ky[:, :DK], ky[:, DK:], jnp.exp(last)))
    return results


MESH = pl.DeviceIdType.MESH


def body(nh, nc, alog_ref, dt_ref, q_hbm, k_hbm, v_hbm, cq_hbm, ck_hbm, cv_hbm, a_hbm, b_hbm,
         gate_hbm, gain_hbm, w_hbm, out_ref,
         q_ref, k_ref, v_ref, cq_ref, ck_ref, cv_ref, a_ref, b_ref, gate_ref, gain_ref, w,
         hq, hk, hv, ext, qe_ref, o_ref, d_ref, g_ref, bb_ref,
         gated, acc, s_in, s_out, f_out, db, pdb, pg, own, p1, r1, p2, r2,
         in_sem, h_send, h_recv, s_send, s_recv, f_send, f_recv, e_send, e_recv, p1_send, p1_recv, p2_send, p2_recv):
    head = lax.axis_index("head")
    ctx = lax.axis_index("ctx")
    nx = nh // 2
    x = head // 2
    core = head % 2
    mate = x * 2 + (1 - core)
    n = q_ref.shape[0]
    khl = q_ref.shape[1] // DK
    vhl = khl * RATIO
    width = out_ref.shape[1]
    peers = [((x + 1 + i) % nx) for i in range(nx)]

    barrier = pltpu.get_barrier_semaphore()
    pl.semaphore_signal(barrier, inc=1, device_id=(mate, ctx), device_id_type=MESH)
    for i in range(nx - 1):
        pl.semaphore_signal(barrier, inc=1, device_id=(peers[i] * 2 + core, ctx), device_id_type=MESH)

    @pl.when(ctx > 0)
    def _():
        pl.semaphore_signal(barrier, inc=1, device_id=(head, ctx - 1), device_id_type=MESH)

    @pl.when(ctx < nc - 1)
    def _():
        pl.semaphore_signal(barrier, inc=1, device_id=(head, ctx + 1), device_id_type=MESH)

    even = ctx % 2 == 0

    @pl.when(jnp.logical_and(even, ctx > 1))
    def _():
        pl.semaphore_signal(barrier, inc=1, device_id=(head, ctx - 2), device_id_type=MESH)

    @pl.when(jnp.logical_and(even, ctx < nc - 2))
    def _():
        pl.semaphore_signal(barrier, inc=1, device_id=(head, ctx + 2), device_id_type=MESH)

    pairs = [
        (q_hbm, q_ref), (k_hbm, k_ref), (v_hbm, v_ref), (cq_hbm, cq_ref), (ck_hbm, ck_ref), (cv_hbm, cv_ref),
        (a_hbm, a_ref), (b_hbm, b_ref), (gate_hbm, gate_ref), (gain_hbm, gain_ref), (w_hbm, w),
    ]
    loads = [pltpu.make_async_copy(src, dst, in_sem.at[i]) for i, (src, dst) in enumerate(pairs)]
    for load in loads:
        load.start()

    neighbours = jnp.minimum(ctx, 1) + jnp.minimum(nc - 1 - ctx, 1)
    seconds = (1 - ctx % 2) * (jnp.minimum(ctx // 2, 1) + jnp.minimum((nc - 1 - ctx) // 2, 1))
    pl.semaphore_wait(barrier, nx + neighbours + seconds)

    halos = [
        pltpu.make_async_remote_copy(
            src_ref=src.at[pl.ds(n - 16, 16)], dst_ref=dst, send_sem=h_send.at[i], recv_sem=h_recv.at[i],
            device_id=(head, ctx + 1), device_id_type=MESH,
        )
        for i, (src, dst) in enumerate([(q_hbm, hq), (k_hbm, hk), (v_hbm, hv)])
    ]

    @pl.when(ctx < nc - 1)
    def _():
        for halo in halos:
            halo.start()

    @pl.when(ctx == 0)
    def _():
        hq[...] = jnp.zeros_like(hq)
        hk[...] = jnp.zeros_like(hk)
        hv[...] = jnp.zeros_like(hv)
        s_in[...] = jnp.zeros_like(s_in)

    for load in loads[:8]:
        load.wait()

    @pl.when(ctx > 0)
    def _():
        for halo in halos:
            halo.wait_recv()

    group = 2 if khl % 2 == 0 else 1
    vw = RATIO * DV

    per_step = group * RATIO

    def pair_copies(step):
        some = pl.ds(step * per_step, per_step)
        return [
            pltpu.make_async_remote_copy(
                src_ref=src.at[some], dst_ref=dst.at[some], send_sem=e_send.at[i, step], recv_sem=e_recv.at[i, step],
                device_id=(head, ctx - 1), device_id_type=MESH,
            )
            for i, (src, dst) in enumerate([(db, pdb), (g_ref, pg)])
        ]

    gives = jnp.logical_and(jnp.logical_not(even), ctx < nc - 1)
    composes = jnp.logical_and(even, ctx < nc - 2)

    def local_step(step, carry):
        heads, lds, strengths = [], [], []
        for t in range(group):
            g = step * group + t
            kc = pl.ds(pl.multiple_of(g * DK, DK), DK)
            vc = pl.ds(pl.multiple_of(g * vw, vw), vw)
            q = unit(conv(q_ref[:, kc], hq[:, kc], cq_ref[:, kc], ext)) * DK ** (-0.5)
            k = unit(conv(k_ref[:, kc], hk[:, kc], ck_ref[:, kc], ext))
            v = conv(v_ref[:, vc], hv[:, vc], cv_ref[:, vc], ext)
            heads.append((q, k, v))
            for r in range(RATIO):
                h = g * RATIO + r
                ax = pick_row(a_ref[...], h) + dt_ref[h]
                rate = jnp.exp(jnp.full((1, n), alog_ref[h], F32))
                lds.append(-rate * (jnp.maximum(ax, 0.0) + jnp.log1p(jnp.exp(-jnp.abs(ax)))))
                strengths.append(1.0 / (1.0 + jnp.exp(-pick_row(b_ref[...], h))))
        terms = local_terms(heads, jnp.concatenate(lds, axis=0), jnp.concatenate(strengths, axis=0))
        for t, (qe, o, d, bb, gl) in enumerate(terms):
            h = step * (group * RATIO) + t
            columns = pl.ds(pl.multiple_of(h * DV, DV), DV)
            qe_ref[:, columns] = qe
            o_ref[:, columns] = o
            d_ref[h] = d
            g_ref[h] = jnp.broadcast_to(gl, (8, DV))
            bb_ref[h] = bb
            db[h] = jnp.concatenate([d, bb], axis=1).astype(BF16)

        @pl.when(gives)
        def _():
            for copy in pair_copies(step):
                copy.start()

        return carry

    lax.fori_loop(0, khl // group, local_step, 0)

    for load in loads[8:10]:
        load.wait()

    def state_copy(h):
        return pltpu.make_async_remote_copy(
            src_ref=s_out.at[h], dst_ref=s_in.at[h], send_sem=s_send.at[h], recv_sem=s_recv.at[h],
            device_id=(head, ctx + 1), device_id_type=MESH,
        )

    def forward_copy(h):
        return pltpu.make_async_remote_copy(
            src_ref=f_out.at[h], dst_ref=s_in.at[h], send_sem=f_send.at[h], recv_sem=f_recv.at[h],
            device_id=(head, ctx + 2), device_id_type=MESH,
        )

    def relay_step(step, carry):
        for copy in pair_copies(step):
            copy.wait_recv()

        for t in range(per_step):
            h = step * per_step + t
            g1 = pg[h][0:1, :]
            later = pdb[h]
            d1 = later[:, :DK]
            both = mm1(d1, db[h])
            pair_d = (g1 * d_ref[h] + g_ref[h][0:1, :] * d1.astype(F32) - both[:, :DK]).astype(BF16)
            pdb[h, :, :DK] = pair_d
            d_ref[h] = later[:, DK:].astype(F32) + g1 * bb_ref[h] - both[:, DK:]

        def relay(t, inner):
            h = step * per_step + t

            @pl.when(ctx > 0)
            def _():
                forward_copy(h).wait_recv()

            state = s_in[h]
            decay = pg[h][0:1, :] * g_ref[h][0:1, :]
            moved = (decay * state.astype(F32) + d_ref[h]) - mm1(pdb[h][:, :DK], state)
            f_out[h] = moved.astype(BF16)
            forward_copy(h).start()
            return inner

        return lax.fori_loop(0, per_step, relay, carry)

    @pl.when(composes)
    def _():
        lax.fori_loop(0, khl // group, relay_step, 0)

    def hand_over(h, carry):
        if nc > 2:
            @pl.when(ctx == nc - 2)
            def _():
                forward_copy(h).wait_recv()

        state = s_in[h]
        moved = (g_ref[h][0:1, :] * state.astype(F32) + bb_ref[h]) - mm1(db[h][:, :DK], state)
        s_out[h] = moved.astype(BF16)
        state_copy(h).start()
        return carry

    @pl.when(even)
    def _():
        lax.fori_loop(0, vhl, hand_over, 0)

    loads[10].wait()

    def finish_pair(p):
        @pl.when(jnp.logical_not(even))
        def _():
            for r in range(RATIO):
                state_copy(p * RATIO + r).wait_recv()

        for r in range(RATIO):
            h = p * RATIO + r
            state = s_in[h]
            columns = pl.ds(h * DV if isinstance(h, int) else pl.multiple_of(h * DV, DV), DV)
            qh, ql = split(qe_ref[:, columns])
            values = o_ref[:, columns] + (mm1(qh, state) + mm1(ql, state))
            scale = lax.rsqrt(jnp.mean(values * values, axis=-1, keepdims=True) + 1e-06)
            gate = silu(gate_ref[:, columns].astype(F32))
            gated[:, r * DV : (r + 1) * DV] = (values * scale * gain_ref[...] * gate).astype(BF16)

    def add_pair(p, carry):
        finish_pair(p)
        rows = pl.ds(pl.multiple_of(p * vw, vw), vw)
        for j in range(nh):
            cols = slice(j * width, (j + 1) * width)
            acc[:, cols] = acc[:, cols] + mm1(gated[...], w[rows, cols])
        return carry

    acc[...] = jnp.zeros_like(acc)
    lax.fori_loop(0, khl - 1, add_pair, 0)
    finish_pair(khl - 1)

    def block(index):
        cols = pl.ds(pl.multiple_of(index * width, 128), width)
        return acc[:, cols] + mm1(gated[...], w[pl.ds((khl - 1) * vw, vw), cols])

    def mate_copy(i):
        return pltpu.make_async_remote_copy(
            src_ref=p1.at[i], dst_ref=r1.at[i], send_sem=p1_send.at[i], recv_sem=p1_recv.at[i],
            device_id=(mate, ctx), device_id_type=MESH,
        )

    def chip_copy(i):
        return pltpu.make_async_remote_copy(
            src_ref=p2.at[i], dst_ref=r2.at[i], send_sem=p2_send.at[i], recv_sem=p2_recv.at[i],
            device_id=(peers[i] * 2 + core, ctx), device_id_type=MESH,
        )

    for i in range(nx):
        p1[i] = block(peers[i] * 2 + (1 - core)).astype(BF16)
        mate_copy(i).start()
    for i in range(nx - 1):
        own[...] = block(peers[i] * 2 + core)
        mate_copy(i).wait_recv()
        p2[i] = (own[...] + r1[i].astype(F32)).astype(BF16)
        chip_copy(i).start()
    own[...] = block(head)
    mate_copy(nx - 1).wait_recv()
    total = own[...] + r1[nx - 1].astype(F32)
    for i in range(nx - 1):
        chip_copy(i).wait_recv()
        total = total + r2[i].astype(F32)
    out_ref[...] = total.astype(BF16)
    for i in range(nx):
        mate_copy(i).wait_send()
    for i in range(nx - 1):
        chip_copy(i).wait_send()

    @pl.when(ctx < nc - 1)
    def _():
        for halo in halos:
            halo.wait_send()

    @pl.when(even)
    def _():
        def drain(h, carry):
            state_copy(h).wait_send()
            return carry

        lax.fori_loop(0, vhl, drain, 0)

    @pl.when(composes)
    def _():
        def drain(h, carry):
            forward_copy(h).wait_send()
            return carry

        lax.fori_loop(0, vhl, drain, 0)

    @pl.when(gives)
    def _():
        for step in range(khl // group):
            for copy in pair_copies(step):
                copy.wait_send()


def local(q_in, k_in, v_in, gate_in, conv_q, conv_k, value_conv_taps, a_in, b_in, a_log, dt_bias,
          norm_gain, out_weight):
    n = q_in.shape[0]
    khl = q_in.shape[1] // DK
    vhl = khl * RATIO
    nh = lax.axis_size("head")
    nc = lax.axis_size("ctx")
    nx = nh // 2
    rows, total_width = out_weight.shape
    width = total_width // nh
    smem = pl.BlockSpec(memory_space=pltpu.SMEM)
    hbm = pl.BlockSpec(memory_space=pltpu.HBM)
    dma = pltpu.SemaphoreType.DMA
    operands = (q_in, k_in, v_in, conv_q, conv_k, value_conv_taps, a_in, b_in, gate_in,
                norm_gain.reshape(1, DV), out_weight)
    vmem = pltpu.VMEM
    return pl.pallas_call(
        functools.partial(body, nh, nc),
        in_specs=[smem, smem] + [hbm] * len(operands),
        out_specs=pl.BlockSpec(memory_space=pltpu.VMEM),
        out_shape=jax.ShapeDtypeStruct((n, width), BF16),
        scratch_shapes=[vmem(op.shape, op.dtype) for op in operands] + [
            vmem((16, q_in.shape[1]), BF16),
            vmem((16, k_in.shape[1]), BF16),
            vmem((16, v_in.shape[1]), BF16),
            vmem((n + 8, RATIO * DV), F32),
            vmem((n, vhl * DK), F32),
            vmem((n, vhl * DV), F32),
            vmem((vhl, DK, DK), F32),
            vmem((vhl, 8, DV), F32),
            vmem((vhl, DK, DV), F32),
            vmem((n, RATIO * DV), BF16),
            vmem((n, total_width), F32),
            vmem((vhl, DK, DV), BF16),
            vmem((vhl, DK, DV), BF16),
            vmem((vhl, DK, DV), BF16),
            vmem((vhl, DK, DK + DV), BF16),
            vmem((vhl, DK, DK + DV), BF16),
            vmem((vhl, 8, DV), F32),
            vmem((n, width), F32),
            vmem((nx, n, width), BF16),
            vmem((nx, n, width), BF16),
            vmem((nx - 1, n, width), BF16),
            vmem((nx - 1, n, width), BF16),
            dma((len(operands),)),
            dma((3,)),
            dma((3,)),
            dma((vhl,)),
            dma((vhl,)),
            dma((vhl,)),
            dma((vhl,)),
            dma((2, khl)),
            dma((2, khl)),
            dma((nx,)),
            dma((nx,)),
            dma((nx - 1,)),
            dma((nx - 1,)),
        ],
        compiler_params=pltpu.CompilerParams(
            collective_id=0, has_side_effects=True, vmem_limit_bytes=63 << 20
        ),
    )(a_log, dt_bias, *operands)


def solution(mesh):
    return jax.shard_map(
        local,
        mesh=mesh,
        in_specs=(
            P("ctx", "head"),
            P("ctx", "head"),
            P("ctx", "head"),
            P("ctx", "head"),
            P(None, "head"),
            P(None, "head"),
            P(None, "head"),
            P("head", "ctx"),
            P("head", "ctx"),
            P("head"),
            P("head"),
            P(),
            P("head", None),
        ),
        out_specs=P("ctx", "head"),
        check_vma=False,
    )
```
